256 devices in a mesh: gx: 8 (over z_lo, y), gy: 8 (over x, core), dir: 4 (over z_hi).
Axes of the slice: x: 4, y: 4, z: 8 (z_hi: 4, z_lo: 2; z = z_hi * 2 + z_lo), core: 2. Of those that a mesh axis runs over, the one named last changes fastest.
Arguments:
- directions: float32 [32, 1024, 2048], P('dir', 'gx', 'gy'), may hold values from -6 to 6
- velocity: float32 [2, 1024, 2048], P(None, 'gx', 'gy'), may hold values from -6 to 6
- viscosity: float32 [1024, 2048], P('gx', 'gy'), may hold values from 0.5 to 2
- basal_drag: float32 [1024, 2048], P('gx', 'gy'), may hold values from 0.5 to 8
- misfit_weight: float32 [1024, 2048], P('gx', 'gy'), may hold values from 1 to 10
- ice_mask: int32 [1024, 2048], P('gx', 'gy'), may hold values 0 or 1
- grounded: int32 [1024, 2048], P('gx', 'gy'), may hold values 0 or 1
Outputs:
- basis: float32 [32, 1024, 2048], P('dir', 'gx', 'gy')
- upper: float32 [32, 32], replicated
The draws below stay inside these ranges and needn't reach their ends.
All inputs are finite; a program needn't handle non-finite values. No bound on the sum of `ice_mask` or of `grounded` on one device may be relied on, other than what follows from the above.
Results may differ from the reference program's by a relative error of at most 0.00021.
Values sent between devices are 32-bit elements; how exact they have to be, the bound alone decides.
A program may use at most 64 MiB of HBM per device.

```python
import math
import jax
import jax.numpy as jnp
from jax import lax

K = 32
SWEEPS = 6
NX = 1024
NY = 2048


def place_ends(values, own_key, smallest, high):
    shape = values.shape
    spot = [jax.random.randint(jax.random.fold_in(own_key, axis), (), 0, shape[axis]) for axis in range(len(shape))]
    values = values.at[tuple(spot)].set(smallest)
    longest = shape.index(max(shape))
    spot[longest] = (spot[longest] + 1) % shape[longest]
    return values.at[tuple(spot)].set(high)


def block_scale(rng, extent, cuts, smallest, high):
    gain = 1.0
    for position, shards_of in cuts:
        heights = jax.random.uniform(jax.random.fold_in(jax.random.fold_in(rng, 6), position), (shards_of,), jnp.float32, smallest / len(cuts), high / len(cuts))
        gain = gain * jnp.repeat(jnp.exp(heights), extent[position] // shards_of).reshape((-1,) + (1,) * (len(extent) - 1 - position))
    return gain


def scatter_about(rng, extent, deviation, most, cuts=(), kind=jnp.bfloat16):
    values = deviation * jax.random.normal(rng, extent, jnp.float32)
    if cuts:
        values = values * block_scale(rng, extent, cuts, -0.22, 0.18)
    return jnp.clip(values, -most, most).astype(kind)


def setup_inputs(seed: int = 0) -> dict:
    key_of = jax.random.split(jax.random.key(seed), 8)
    directions = scatter_about(key_of[0], (K, NX, NY), 1.0, 6.0, ((0, 4), (1, 8), (2, 8)), jnp.float32)
    velocity = scatter_about(key_of[1], (2, NX, NY), 1.0, 6.0, ((1, 8), (2, 8)), jnp.float32)
    viscosity = jnp.clip(jnp.exp(math.log(2.0) - 1.3862944 * jax.random.uniform(key_of[2], (NX, NY), jnp.float32) ** block_scale(key_of[2], (NX, NY), ((0, 8), (1, 8)), -0.2, 0.2)), 0.5, 2.0)
    basal_drag = jnp.clip(jnp.exp(math.log(8.0) - 2.7725887 * jax.random.uniform(key_of[3], (NX, NY), jnp.float32) ** block_scale(key_of[3], (NX, NY), ((0, 8), (1, 8)), -0.2, 0.2)), 0.5, 8.0)
    misfit_weight = jnp.clip(jnp.exp(math.log(10.0) - 2.3025851 * jax.random.uniform(key_of[4], (NX, NY), jnp.float32) ** block_scale(key_of[4], (NX, NY), ((0, 8), (1, 8)), -0.2, 0.2)), 1.0, 10.0)
    ice_mask = place_ends((jax.random.randint(key_of[5], (NX, NY), 0, 16) < 15).astype(jnp.int32), jax.random.fold_in(key_of[5], 1), 0, 1)
    grounded = place_ends((jax.random.randint(key_of[6], (NX, NY), 0, 2) < 1).astype(jnp.int32), jax.random.fold_in(key_of[6], 1), 0, 1)
    return {"directions": directions, "velocity": velocity, "viscosity": viscosity, "basal_drag": basal_drag, "misfit_weight": misfit_weight, "ice_mask": ice_mask, "grounded": grounded}


damping = 0.8

def face_terms(viscosity):
    padded = jnp.pad(viscosity, 1)
    face_east = 0.5 * (viscosity + padded[2:, 1:-1])
    face_west = 0.5 * (viscosity + padded[:-2, 1:-1])
    face_north = 0.5 * (viscosity + padded[1:-1, 2:])
    face_south = 0.5 * (viscosity + padded[1:-1, :-2])
    return (face_east, face_west, face_north, face_south)

def weights_pair():
    along_x = jnp.array([4.0, 1.0], jnp.float32).reshape(2, 1, 1)
    along_y = jnp.array([1.0, 4.0], jnp.float32).reshape(2, 1, 1)
    return (along_x, along_y)

def relax_sweep(state, padded, coeffs, source):
    face_east, face_west, face_north, face_south, friction, diagonal, ice_keep = coeffs
    along_x, along_y = weights_pair()
    next_row = padded[..., 2:, 1:-1]
    prev_row = padded[..., :-2, 1:-1]
    next_col = padded[..., 1:-1, 2:]
    prev_col = padded[..., 1:-1, :-2]
    applied = along_x * (face_east * (state - next_row) + face_west * (state - prev_row))
    applied = applied + along_y * (face_north * (state - next_col) + face_south * (state - prev_col))
    applied = applied + friction * state
    return ice_keep * (state + damping * (source - applied) / diagonal)

def solve_field(source, coeffs):
    diagonal, ice_keep = (coeffs[5], coeffs[6])
    state = ice_keep * damping * source / diagonal
    for sweep in range(SWEEPS - 1):
        padded = jnp.pad(state, ((0, 0), (1, 1), (1, 1)))
        state = relax_sweep(state, padded, coeffs, source)
    return state

def reference(directions, velocity, viscosity, basal_drag, misfit_weight, ice_mask, grounded):
    face_east, face_west, face_north, face_south = face_terms(viscosity)
    friction = basal_drag * grounded.astype(jnp.float32)
    ice_keep = ice_mask.astype(jnp.float32)
    along_x, along_y = weights_pair()
    diagonal = along_x * (face_east + face_west) + along_y * (face_north + face_south) + friction
    coeffs = (face_east, face_west, face_north, face_south, friction, diagonal, ice_keep)

    def one_direction(direction):
        forward = solve_field(-friction * velocity * direction, coeffs)
        adjoint = solve_field(misfit_weight * forward, coeffs)
        return -friction * jnp.sum(velocity * adjoint, axis=0)
    sketch = lax.map(one_direction, directions)
    flat = sketch.reshape(K, NX * NY)
    gram = jnp.dot(flat.astype(jnp.float32), flat.T.astype(jnp.float32), precision=lax.Precision.HIGHEST, preferred_element_type=jnp.float32)
    gram = gram / jnp.float32(NX * NY)
    lower = jnp.linalg.cholesky(gram)
    inverse = lax.linalg.triangular_solve(lower, jnp.eye(K, dtype=jnp.float32), left_side=True, lower=True)
    basis = jnp.dot(inverse.astype(jnp.float32), flat.astype(jnp.float32), precision=lax.Precision.HIGHEST, preferred_element_type=jnp.float32)
    return (basis.reshape(K, NX, NY), lower.T)
```

```python
import functools

import jax
import jax.numpy as jnp
from jax import lax
from jax.experimental import pallas as pl
from jax.experimental.pallas import tpu as pltpu
from jax.sharding import PartitionSpec as P

SWEEPS = 6
DAMPING = 0.8
HR = 16
HC = 16
AX = (4.0, 1.0)
AY = (1.0, 4.0)
LEVELS = 2 * (SWEEPS - 1)
CHUNKS = 4
MESH = pl.DeviceIdType.MESH
F32 = jnp.float32
BF16 = jnp.bfloat16
VEL, VISC, FRIC, MISFIT, KEEP = 0, 2, 3, 4, 5
CE, CW, CN, CS, SB, GM, CQ = range(0, 14, 2)


def split(x):
    hi = x.astype(BF16)
    lo = (x - hi.astype(F32)).astype(BF16)
    return hi, lo


def dot(a, b, contract):
    return lax.dot_general(a, b, ((contract[:1], contract[1:]), ((), ())), preferred_element_type=F32)


def kernel(
    sizes,
    dirs_hbm,
    vel_hbm,
    visc_hbm,
    drag_hbm,
    misfit_hbm,
    mask_hbm,
    ground_hbm,
    out_hbm,
    upper_ref,
    fld,
    fldc,
    dr,
    drc,
    raw,
    rawi,
    pks,
    pkr,
    co,
    w,
    sk,
    rx,
    gs,
    gr,
    ob,
    in_sem,
    row_send,
    row_recv,
    col_send,
    col_recv,
    a2a_send,
    a2a_recv,
    own_sem,
    ar_send,
    ar_recv,
    ret_send,
    ret_recv,
    ret_own,
):
    gx_n, gy_n, nd, rows, total = sizes
    full = rows + 2 * HR
    blocks = full // 8
    chunk = rows // CHUNKS
    quarter = chunk // nd
    kk = 8 * nd
    gx, gy, me = (lax.axis_index(a) for a in ("gx", "gy", "dir"))
    lane = lax.broadcasted_iota(jnp.int32, (8, 128), 1)

    barrier = pltpu.get_barrier_semaphore()
    peers = 0
    for axis, index, count in (("gx", gx, gx_n), ("gy", gy, gy_n), ("dir", me, nd)):
        for o in range(1, count):
            pl.semaphore_signal(
                barrier, inc=1, device_id={axis: lax.rem(index + o, count)}, device_id_type=MESH
            )
            peers += 1

    dr4 = dr.reshape(2, 8, full, 128)
    body = pl.ds(HR, rows)
    loads = []
    for t in range(2):
        cols = pl.ds(128 * t, 128)
        loads += [
            (vel_hbm.at[:, :, cols], fld.at[0:2, t, body, :]),
            (visc_hbm.at[:, cols], fld.at[VISC, t, body, :]),
            (misfit_hbm.at[:, cols], fld.at[MISFIT, t, body, :]),
            (drag_hbm.at[:, cols], raw.at[t]),
            (mask_hbm.at[:, cols], rawi.at[0, t]),
            (ground_hbm.at[:, cols], rawi.at[1, t]),
            (dirs_hbm.at[:, :, cols], dr4.at[t, :, body, :]),
        ]
    copies = [pltpu.make_async_copy(s, d, in_sem.at[i]) for i, (s, d) in enumerate(loads)]
    for c in copies:
        c.start()

    def zero_rows(start):
        z = jnp.zeros((HR, 128), F32)
        for t in range(2):
            for p in range(6):
                fld[p, t, pl.ds(start, HR), :] = z
            for k in range(8):
                dr[t, pl.ds(k * full + start, HR), :] = z

    @pl.when(gx == 0)
    def _():
        zero_rows(0)

    @pl.when(gx == gx_n - 1)
    def _():
        zero_rows(HR + rows)

    @pl.when(gy == 0)
    def _():
        pkr[:, 0] = jnp.zeros((2, full, 128), F32)

    @pl.when(gy == gy_n - 1)
    def _():
        pkr[:, 1] = jnp.zeros((2, full, 128), F32)

    for c in copies:
        c.wait()
    for t in range(2):
        fld[FRIC, t, body, :] = raw[t] * rawi[1, t].astype(F32)
        fld[KEEP, t, body, :] = rawi[0, t].astype(F32)
    pl.semaphore_wait(barrier, peers)

    top, bottom = pl.ds(HR, HR), pl.ds(rows, HR)
    above, below = pl.ds(0, HR), pl.ds(HR + rows, HR)

    def row_copy(kind, up):
        src, dst = (top, below) if up else (bottom, above)
        ref = (fld, dr4)[kind]
        peer = lax.rem(gx + (gx_n - 1 if up else 1), gx_n)
        return pltpu.make_async_remote_copy(
            src_ref=ref.at[:, :, src, :],
            dst_ref=ref.at[:, :, dst, :],
            send_sem=row_send.at[kind, int(up)],
            recv_sem=row_recv.at[kind, int(up)],
            device_id={"gx": peer},
            device_id_type=MESH,
        )

    has_up, has_down = gx > 0, gx < gx_n - 1
    for kind in range(2):

        @pl.when(has_up)
        def _():
            row_copy(kind, True).start()

        @pl.when(has_down)
        def _():
            row_copy(kind, False).start()

    def col_copy(kind, left):
        peer = lax.rem(gy + (gy_n - 1 if left else 1), gy_n)
        return pltpu.make_async_remote_copy(
            src_ref=pks.at[kind, 0 if left else 1],
            dst_ref=pkr.at[kind, 1 if left else 0],
            send_sem=col_send.at[kind, int(left)],
            recv_sem=col_recv.at[kind, int(left)],
            device_id={"gy": peer},
            device_id_type=MESH,
        )

    has_left, has_right = gy > 0, gy < gy_n - 1

    def plane(kind, p, t, at):
        if kind == 0:
            return fld[p, t, at, :]
        return dr[t, pl.ds(pl.multiple_of(p * full + at.start, 8), 8), :]

    for kind in range(2):
        count = (6, 8)[kind]

        @pl.when(has_down)
        def _():
            row_copy(kind, True).wait_recv()

        @pl.when(has_up)
        def _():
            row_copy(kind, False).wait_recv()

        def pack(i, _):
            at = pl.ds(pl.multiple_of(8 * i, 8), 8)
            to_left = jnp.zeros((8, 128), F32)
            to_right = jnp.zeros((8, 128), F32)
            for p in range(count):
                here = (lane >= HC * p) & (lane < HC * (p + 1))
                first = plane(kind, p, 0, at)
                last = plane(kind, p, 1, at)
                if p:
                    first = pltpu.roll(first, HC * p, axis=1)
                if p != 7:
                    last = pltpu.roll(last, (HC * p - (128 - HC)) % 128, axis=1)
                to_left = jnp.where(here, first, to_left)
                to_right = jnp.where(here, last, to_right)
            pks[kind, 0, at, :] = to_left
            pks[kind, 1, at, :] = to_right
            return 0

        lax.fori_loop(0, blocks, pack, 0)

        @pl.when(has_left)
        def _():
            col_copy(kind, True).start()

        @pl.when(has_right)
        def _():
            col_copy(kind, False).start()

    def unpack(kind):
        count = (6, 8)[kind]

        @pl.when(has_right)
        def _():
            col_copy(kind, True).wait_recv()

        @pl.when(has_left)
        def _():
            col_copy(kind, False).wait_recv()

        def one(i, _):
            at = pl.ds(pl.multiple_of(8 * i, 8), 8)
            left = pkr[kind, 0, at, :]
            right = pkr[kind, 1, at, :]
            for p in range(count):
                r = right if p == 0 else pltpu.roll(right, 128 - HC * p, axis=1)
                l = left if p == 7 else pltpu.roll(left, 128 - HC * (p + 1), axis=1)
                v = jnp.where(lane < HC, r, jnp.where(lane >= 128 - HC, l, 0.0))
                if kind == 0:
                    fldc[p, at, :] = v
                else:
                    drc[pl.ds(pl.multiple_of(p * full + 8 * i, 8), 8), :] = v
            return 0

        lax.fori_loop(0, blocks, one, 0)

    unpack(0)

    def around(tiles):
        nxt = [pltpu.roll(x, 127, axis=1) for x in tiles]
        prv = [pltpu.roll(x, 1, axis=1) for x in tiles]
        after = [jnp.where(lane == 127, nxt[(t + 1) % 3], nxt[t]) for t in range(3)]
        before = [jnp.where(lane == 0, prv[(t + 2) % 3], prv[t]) for t in range(3)]
        return before, after

    def coefficients(i, _):
        at = pl.ds(pl.multiple_of(8 * i, 8), 8)
        at_up = pl.ds(pl.multiple_of(8 * lax.rem(i + blocks - 1, blocks), 8), 8)
        at_down = pl.ds(pl.multiple_of(8 * lax.rem(i + 1, blocks), 8), 8)

        def field(p, rows_at):
            return [fld[p, 0, rows_at, :], fld[p, 1, rows_at, :], fldc[p, rows_at, :]]

        sub = lax.broadcasted_iota(jnp.int32, (8, 128), 0)
        visc = field(VISC, at)
        up, down = field(VISC, at_up), field(VISC, at_down)
        before, after = around(visc)
        fric, misfit, keep = field(FRIC, at), field(MISFIT, at), field(KEEP, at)
        vel = [field(VEL, at), field(VEL + 1, at)]
        for t in range(3):
            v = visc[t]
            below_row = jnp.where(sub == 7, pltpu.roll(down[t], 7, axis=0), pltpu.roll(v, 7, axis=0))
            above_row = jnp.where(sub == 0, pltpu.roll(up[t], 1, axis=0), pltpu.roll(v, 1, axis=0))
            east, west = 0.5 * (v + below_row), 0.5 * (v + above_row)
            north, south = 0.5 * (v + after[t]), 0.5 * (v + before[t])
            for c in range(2):
                diagonal = AX[c] * (east + west) + AY[c] * (north + south) + fric[t]
                g = (DAMPING * keep[t]) / jnp.where(keep[t] > 0.0, diagonal, 1.0)
                gx_, gy_ = AX[c] * g, AY[c] * g
                q = -fric[t] * vel[c][t]
                co[CE + c, t, at, :] = gx_ * east
                co[CW + c, t, at, :] = gx_ * west
                co[CN + c, t, at, :] = gy_ * north
                co[CS + c, t, at, :] = gy_ * south
                co[SB + c, t, at, :] = g * q
                co[GM + c, t, at, :] = g * misfit[t]
                co[CQ + c, t, at, :] = q
        return 0

    lax.fori_loop(0, blocks, coefficients, 0)
    unpack(1)

    def coef(p, t, r):
        return jnp.broadcast_to(co[p, t, pl.ds(r, 1), :], (8, 128))

    def first_level(r):
        for t in range(3):
            d = (dr[t, pl.ds(r, 8, stride=full), :] if t < 2 else drc[pl.ds(r, 8, stride=full), :])
            for c in range(2):
                w[0, r, 3 * c + t] = coef(SB + c, t, r) * d

    def level_rows(level, r0, count):
        local = (level - 1) % (SWEEPS - 1) + 1
        src = 0 if local == 1 else 1 + local % 2
        dst = 1 + (local + 1) % 2
        last = level == LEVELS
        half = local == SWEEPS - 1 and not last
        tiles = range(2) if last else range(3)
        sums = [[None, None] for _ in range(count)]
        for c in range(2):
            state = [[w[src, r0 + j, 3 * c + t] for t in range(3)] for j in range(-1, count + 1)]
            for j in range(count):
                r = r0 + j
                up, here, down = state[j], state[j + 1], state[j + 2]
                before, after = around(here)
                for t in tiles:
                    new = 0.2 * here[t] + w[0, r, 3 * c + t]
                    new = new + coef(CE + c, t, r) * down[t] + coef(CW + c, t, r) * up[t]
                    new = new + (coef(CN + c, t, r) * after[t] + coef(CS + c, t, r) * before[t])
                    if last:
                        term = coef(CQ + c, t, r) * new
                        sums[j][t] = term if c == 0 else sums[j][t] + term
                    elif half:
                        w[0, r, 3 * c + t] = coef(GM + c, t, r) * new
                    else:
                        w[dst, r, 3 * c + t] = new
        if last:
            for j in range(count):
                for t in range(2):
                    sk[r0 + j - HR, t] = sums[j][t]

    def a2a_copy(c, o):
        peer = lax.rem(me + o, nd)
        return pltpu.make_async_remote_copy(
            src_ref=sk.at[pl.ds(c * chunk + peer * quarter, quarter)],
            dst_ref=rx.at[me, pl.ds(c * quarter, quarter)],
            send_sem=a2a_send.at[c, o],
            recv_sem=a2a_recv.at[c, o],
            device_id={"dir": peer},
            device_id_type=MESH,
        )

    def own_copy(c):
        return pltpu.make_async_copy(
            sk.at[pl.ds(c * chunk + me * quarter, quarter)],
            rx.at[me, pl.ds(c * quarter, quarter)],
            own_sem.at[c],
        )

    base = HR + LEVELS

    def do_chunk(c, _):
        first = 1 - (c + CHUNKS) // (CHUNKS + 1)
        for level in range(LEVELS + 1):
            stop = base - level + chunk * c
            lo = stop - chunk + first * (chunk - 2 * LEVELS + 2 * level)

            def step(i, _):
                if level == 0:
                    first_level(lo + 2 * i)
                    first_level(lo + 2 * i + 1)
                else:
                    level_rows(level, lo + 2 * i, 2)
                return 0

            lax.fori_loop(0, (stop - lo) // 2, step, 0)

        @pl.when(c > 0)
        def _():
            for o in range(1, nd):
                a2a_copy(c - 1, o).start()
            own_copy(c - 1).start()

        return 0

    lax.fori_loop(0, CHUNKS + 1, do_chunk, 0)

    def gathered(r):
        return [
            jnp.concatenate([rx[g, r, t] for g in range(nd)], axis=0) for t in range(2)
        ]

    def gram_chunk(c, acc):
        for o in range(1, nd):
            a2a_copy(c, o).wait_recv()
        own_copy(c).wait()

        def one(i, acc):
            for x in gathered(c * quarter + i):
                hi, lo = split(x)
                both = jnp.concatenate([hi, lo], axis=0)
                acc = acc + dot(both, both, (1, 1))
            return acc

        return lax.fori_loop(0, quarter, one, acc)

    acc = lax.fori_loop(0, CHUNKS, gram_chunk, jnp.zeros((2 * kk, 2 * kk), F32))
    acc = acc[:kk] + acc[kk:]
    gram = acc[:, :kk] + acc[:, kk:]
    gram = jnp.concatenate([gram, jnp.zeros((kk, 128 - kk), F32)], axis=1)

    def reduce_copy(s, axis, index, count, o):
        return pltpu.make_async_remote_copy(
            src_ref=gs.at[s],
            dst_ref=gr.at[s, index],
            send_sem=ar_send.at[s, o],
            recv_sem=ar_recv.at[s, o],
            device_id={axis: lax.rem(index + o, count)},
            device_id_type=MESH,
        )

    for s, (axis, index, count) in enumerate((("dir", me, nd), ("gy", gy, gy_n), ("gx", gx, gx_n))):
        gs[s] = gram
        gr[s, index] = gram
        for o in range(1, count):
            reduce_copy(s, axis, index, count, o).start()
        for o in range(1, count):
            reduce_copy(s, axis, index, count, o).wait_recv()
        gram = gr[s, 0]
        for j in range(1, count):
            gram = gram + gr[s, j]
    gram = gram / jnp.float32(total)

    line = lax.broadcasted_iota(jnp.int32, (kk, 128), 0)
    place = lax.broadcasted_iota(jnp.int32, (kk, 128), 1)
    m = jnp.where(place == line + kk, 1.0, gram)
    for k in range(kk - 1):
        column = jnp.broadcast_to(m[:, k : k + 1], (kk, 128))
        row = jnp.broadcast_to(m[k : k + 1, :], (kk, 128))
        pivot = jnp.broadcast_to(column[k : k + 1, :], (kk, 128))
        m = m - jnp.where(line > k, column, 0.0) * (row / pivot)
    diag = jnp.sum(jnp.where(place == line, m, 0.0), axis=1, keepdims=True)
    m = m * lax.rsqrt(diag)
    upper_ref[...] = jnp.where(place >= line, m, 0.0)[:, :kk]
    inverse = m[:, kk : 2 * kk]
    inv_hi, inv_lo = split(inverse)
    left = jnp.concatenate(
        [jnp.concatenate([inv_hi, inv_hi], axis=1), jnp.concatenate([inv_lo, inv_lo], axis=1)], axis=0
    )

    def ret_copy(c, o):
        peer = lax.rem(me + o, nd)
        return pltpu.make_async_remote_copy(
            src_ref=ob.at[peer, c],
            dst_ref=out_hbm.at[:, :, pl.ds(c * chunk + me * quarter, quarter), :],
            send_sem=ret_send.at[c, o],
            recv_sem=ret_recv.at[c, o],
            device_id={"dir": peer},
            device_id_type=MESH,
        )

    def ret_own_copy(c):
        return pltpu.make_async_copy(
            ob.at[me, c],
            out_hbm.at[:, :, pl.ds(c * chunk + me * quarter, quarter), :],
            ret_own.at[c],
        )

    def basis_chunk(c, _):
        def one(i, _):
            for t, x in enumerate(gathered(c * quarter + i)):
                hi, lo = split(x)
                out = dot(left, jnp.concatenate([hi, lo], axis=0), (1, 0))
                out = out[:kk] + out[kk:]
                for g in range(nd):
                    flat = ob.at[g, c, t].reshape(8 * quarter, 128)
                    flat[pl.ds(i, 8, stride=quarter), :] = out[8 * g : 8 * g + 8]
            return 0

        lax.fori_loop(0, quarter, one, 0)
        for o in range(1, nd):
            ret_copy(c, o).start()
        ret_own_copy(c).start()
        return 0

    lax.fori_loop(0, CHUNKS, basis_chunk, 0)

    for kind in range(2):

        @pl.when(has_up)
        def _():
            row_copy(kind, True).wait_send()

        @pl.when(has_down)
        def _():
            row_copy(kind, False).wait_send()

        @pl.when(has_left)
        def _():
            col_copy(kind, True).wait_send()

        @pl.when(has_right)
        def _():
            col_copy(kind, False).wait_send()

    for s, (axis, index, count) in enumerate((("dir", me, nd), ("gy", gy, gy_n), ("gx", gx, gx_n))):
        for o in range(1, count):
            reduce_copy(s, axis, index, count, o).wait_send()

    def finish(c, _):
        for o in range(1, nd):
            a2a_copy(c, o).wait_send()
            ret_copy(c, o).wait_send()
            ret_copy(c, o).wait_recv()
        ret_own_copy(c).wait()
        return 0

    lax.fori_loop(0, CHUNKS, finish, 0)


def on_device(mesh, directions, velocity, viscosity, basal_drag, misfit_weight, ice_mask, grounded):
    gx_n, gy_n, nd = (mesh.shape[a] for a in ("gx", "gy", "dir"))
    own, rows, cols = directions.shape
    full = rows + 2 * HR
    chunk = rows // CHUNKS
    quarter = chunk // nd
    kk = own * nd
    total = rows * cols * gx_n * gy_n
    most = max(gx_n, gy_n, nd)
    any_space = pl.BlockSpec(memory_space=pl.ANY)
    dma = pltpu.SemaphoreType.DMA
    vmem = pltpu.VMEM
    out, upper = pl.pallas_call(
        functools.partial(kernel, (gx_n, gy_n, nd, rows, total)),
        out_shape=(
            jax.ShapeDtypeStruct((2, own, rows, 128), F32),
            jax.ShapeDtypeStruct((kk, kk), F32),
        ),
        in_specs=[any_space] * 7,
        out_specs=(any_space, pl.BlockSpec(memory_space=pltpu.VMEM)),
        scratch_shapes=[
            vmem((6, 2, full, 128), F32),
            vmem((6, full, 128), F32),
            vmem((2, 8 * full, 128), F32),
            vmem((8 * full, 128), F32),
            vmem((2, rows, 128), F32),
            vmem((2, 2, rows, 128), jnp.int32),
            vmem((2, 2, full, 128), F32),
            vmem((2, 2, full, 128), F32),
            vmem((14, 3, full, 128), F32),
            vmem((3, full, 6, 8, 128), F32),
            vmem((rows, 2, 8, 128), F32),
            vmem((nd, rows // nd, 2, 8, 128), F32),
            vmem((3, kk, 128), F32),
            vmem((3, most, kk, 128), F32),
            vmem((nd, CHUNKS, 2, 8, quarter, 128), F32),
            dma((14,)),
            dma((2, 2)),
            dma((2, 2)),
            dma((2, 2)),
            dma((2, 2)),
            dma((CHUNKS, nd)),
            dma((CHUNKS, nd)),
            dma((CHUNKS,)),
            dma((3, most)),
            dma((3, most)),
            dma((CHUNKS, nd)),
            dma((CHUNKS, nd)),
            dma((CHUNKS,)),
        ],
        compiler_params=pltpu.CompilerParams(
            collective_id=0, has_side_effects=True, vmem_limit_bytes=48 << 20
        ),
        name="sketch",
    )(directions, velocity, viscosity, basal_drag, misfit_weight, ice_mask, grounded)
    return out.transpose(1, 2, 0, 3).reshape(own, rows, cols), upper


def solution(mesh):
    placed = (P("dir", "gx", "gy"), P(None, "gx", "gy")) + (P("gx", "gy"),) * 5
    return jax.shard_map(
        functools.partial(on_device, mesh),
        mesh=mesh,
        in_specs=placed,
        out_specs=(P("dir", "gx", "gy"), P()),
        check_vma=False,
    )
```

```python
import functools

import jax
import jax.numpy as jnp
from jax import lax
from jax.experimental import pallas as pl
from jax.experimental.pallas import tpu as pltpu
from jax.sharding import PartitionSpec as P

SWEEPS = 6
DAMPING = 0.8
HR = 16
HC = 16
AX = (4.0, 1.0)
AY = (1.0, 4.0)
LEVELS = 2 * (SWEEPS - 1)
CHUNKS = 4
STEP = 8
MESH = pl.DeviceIdType.MESH
F32 = jnp.float32
BF16 = jnp.bfloat16
VEL, VISC, FRIC, MISFIT, KEEP = 0, 2, 3, 4, 5
CE, CW, CN, CS, SB, GM, CQ = range(0, 14, 2)


def split(x):
    hi = x.astype(BF16)
    lo = (x - hi.astype(F32)).astype(BF16)
    return hi, lo


def dot(a, b, contract):
    return lax.dot_general(a, b, ((contract[:1], contract[1:]), ((), ())), preferred_element_type=F32)


def kernel(
    sizes,
    dirs_hbm,
    vel_hbm,
    visc_hbm,
    drag_hbm,
    misfit_hbm,
    mask_hbm,
    ground_hbm,
    out_hbm,
    upper_ref,
    fld,
    fldc,
    dr,
    drc,
    raw,
    rawi,
    pks,
    pkr,
    co,
    w,
    sk,
    rx,
    gs,
    gr,
    ob,
    in_sem,
    row_send,
    row_recv,
    col_send,
    col_recv,
    a2a_send,
    a2a_recv,
    own_sem,
    ar_send,
    ar_recv,
    ret_send,
    ret_recv,
    ret_own,
):
    gx_n, gy_n, nd, rows, total = sizes
    full = rows + 2 * HR
    blocks = full // 8
    chunk = rows // CHUNKS
    quarter = chunk // nd
    kk = 8 * nd
    gx, gy, me = (lax.axis_index(a) for a in ("gx", "gy", "dir"))
    lane = lax.broadcasted_iota(jnp.int32, (8, 128), 1)

    barrier = pltpu.get_barrier_semaphore()
    peers = 0
    for axis, index, count in (("gx", gx, gx_n), ("gy", gy, gy_n), ("dir", me, nd)):
        for o in range(1, count):
            pl.semaphore_signal(
                barrier, inc=1, device_id={axis: lax.rem(index + o, count)}, device_id_type=MESH
            )
            peers += 1

    dr4 = dr.reshape(2, 8, full, 128)
    body = pl.ds(HR, rows)
    loads = []
    for t in range(2):
        cols = pl.ds(128 * t, 128)
        loads += [
            (vel_hbm.at[:, :, cols], fld.at[0:2, t, body, :]),
            (visc_hbm.at[:, cols], fld.at[VISC, t, body, :]),
            (misfit_hbm.at[:, cols], fld.at[MISFIT, t, body, :]),
            (drag_hbm.at[:, cols], raw.at[t]),
            (mask_hbm.at[:, cols], rawi.at[0, t]),
            (ground_hbm.at[:, cols], rawi.at[1, t]),
            (dirs_hbm.at[:, :, cols], dr4.at[t, :, body, :]),
        ]
    copies = [pltpu.make_async_copy(s, d, in_sem.at[i]) for i, (s, d) in enumerate(loads)]
    for c in copies:
        c.start()

    def zero_rows(start):
        z = jnp.zeros((HR, 128), F32)
        for t in range(2):
            for p in range(6):
                fld[p, t, pl.ds(start, HR), :] = z
            for k in range(8):
                dr[t, pl.ds(k * full + start, HR), :] = z

    @pl.when(gx == 0)
    def _():
        zero_rows(0)

    @pl.when(gx == gx_n - 1)
    def _():
        zero_rows(HR + rows)

    @pl.when(gy == 0)
    def _():
        pkr[:, 0] = jnp.zeros((2, full, 128), F32)

    @pl.when(gy == gy_n - 1)
    def _():
        pkr[:, 1] = jnp.zeros((2, full, 128), F32)

    for c in copies:
        c.wait()
    for t in range(2):
        fld[FRIC, t, body, :] = raw[t] * rawi[1, t].astype(F32)
        fld[KEEP, t, body, :] = rawi[0, t].astype(F32)
    pl.semaphore_wait(barrier, peers)

    top, bottom = pl.ds(HR, HR), pl.ds(rows, HR)
    above, below = pl.ds(0, HR), pl.ds(HR + rows, HR)

    def row_copy(kind, up):
        src, dst = (top, below) if up else (bottom, above)
        ref = (fld, dr4)[kind]
        peer = lax.rem(gx + (gx_n - 1 if up else 1), gx_n)
        return pltpu.make_async_remote_copy(
            src_ref=ref.at[:, :, src, :],
            dst_ref=ref.at[:, :, dst, :],
            send_sem=row_send.at[kind, int(up)],
            recv_sem=row_recv.at[kind, int(up)],
            device_id={"gx": peer},
            device_id_type=MESH,
        )

    has_up, has_down = gx > 0, gx < gx_n - 1
    for kind in range(2):

        @pl.when(has_up)
        def _():
            row_copy(kind, True).start()

        @pl.when(has_down)
        def _():
            row_copy(kind, False).start()

    def col_copy(kind, left):
        peer = lax.rem(gy + (gy_n - 1 if left else 1), gy_n)
        return pltpu.make_async_remote_copy(
            src_ref=pks.at[kind, 0 if left else 1],
            dst_ref=pkr.at[kind, 1 if left else 0],
            send_sem=col_send.at[kind, int(left)],
            recv_sem=col_recv.at[kind, int(left)],
            device_id={"gy": peer},
            device_id_type=MESH,
        )

    has_left, has_right = gy > 0, gy < gy_n - 1

    def plane(kind, p, t, at):
        if kind == 0:
            return fld[p, t, at, :]
        return dr[t, pl.ds(pl.multiple_of(p * full + at.start, 8), 8), :]

    for kind in range(2):
        count = (6, 8)[kind]

        @pl.when(has_down)
        def _():
            row_copy(kind, True).wait_recv()

        @pl.when(has_up)
        def _():
            row_copy(kind, False).wait_recv()

        def pack(i, _):
            at = pl.ds(pl.multiple_of(8 * i, 8), 8)
            to_left = jnp.zeros((8, 128), F32)
            to_right = jnp.zeros((8, 128), F32)
            for p in range(count):
                here = (lane >= HC * p) & (lane < HC * (p + 1))
                first = plane(kind, p, 0, at)
                last = plane(kind, p, 1, at)
                if p:
                    first = pltpu.roll(first, HC * p, axis=1)
                if p != 7:
                    last = pltpu.roll(last, (HC * p - (128 - HC)) % 128, axis=1)
                to_left = jnp.where(here, first, to_left)
                to_right = jnp.where(here, last, to_right)
            pks[kind, 0, at, :] = to_left
            pks[kind, 1, at, :] = to_right
            return 0

        lax.fori_loop(0, blocks // 4, lambda i, x: [pack(4 * i + j, x) for j in range(4)][0], 0)

        @pl.when(has_left)
        def _():
            col_copy(kind, True).start()

        @pl.when(has_right)
        def _():
            col_copy(kind, False).start()

    def unpack(kind):
        count = (6, 8)[kind]

        @pl.when(has_right)
        def _():
            col_copy(kind, True).wait_recv()

        @pl.when(has_left)
        def _():
            col_copy(kind, False).wait_recv()

        def one(i, _):
            at = pl.ds(pl.multiple_of(8 * i, 8), 8)
            left = pkr[kind, 0, at, :]
            right = pkr[kind, 1, at, :]
            for p in range(count):
                r = right if p == 0 else pltpu.roll(right, 128 - HC * p, axis=1)
                l = left if p == 7 else pltpu.roll(left, 128 - HC * (p + 1), axis=1)
                v = jnp.where(lane < HC, r, jnp.where(lane >= 128 - HC, l, 0.0))
                if kind == 0:
                    fldc[p, at, :] = v
                else:
                    drc[pl.ds(pl.multiple_of(p * full + 8 * i, 8), 8), :] = v
            return 0

        lax.fori_loop(0, blocks // 4, lambda i, x: [one(4 * i + j, x) for j in range(4)][0], 0)

    unpack(0)

    def around(tiles):
        nxt = [pltpu.roll(x, 127, axis=1) for x in tiles]
        prv = [pltpu.roll(x, 1, axis=1) for x in tiles]
        after = [jnp.where(lane == 127, nxt[(t + 1) % 3], nxt[t]) for t in range(3)]
        before = [jnp.where(lane == 0, prv[(t + 2) % 3], prv[t]) for t in range(3)]
        return before, after

    def coefficients(i, _):
        at = pl.ds(pl.multiple_of(8 * i, 8), 8)
        at_up = pl.ds(pl.multiple_of(8 * lax.rem(i + blocks - 1, blocks), 8), 8)
        at_down = pl.ds(pl.multiple_of(8 * lax.rem(i + 1, blocks), 8), 8)

        def field(p, rows_at):
            return [fld[p, 0, rows_at, :], fld[p, 1, rows_at, :], fldc[p, rows_at, :]]

        sub = lax.broadcasted_iota(jnp.int32, (8, 128), 0)
        visc = field(VISC, at)
        up, down = field(VISC, at_up), field(VISC, at_down)
        before, after = around(visc)
        fric, misfit, keep = field(FRIC, at), field(MISFIT, at), field(KEEP, at)
        vel = [field(VEL, at), field(VEL + 1, at)]
        for t in range(3):
            v = visc[t]
            below_row = jnp.where(sub == 7, pltpu.roll(down[t], 7, axis=0), pltpu.roll(v, 7, axis=0))
            above_row = jnp.where(sub == 0, pltpu.roll(up[t], 1, axis=0), pltpu.roll(v, 1, axis=0))
            east, west = 0.5 * (v + below_row), 0.5 * (v + above_row)
            north, south = 0.5 * (v + after[t]), 0.5 * (v + before[t])
            for c in range(2):
                diagonal = AX[c] * (east + west) + AY[c] * (north + south) + fric[t]
                g = (DAMPING * keep[t]) / jnp.where(keep[t] > 0.0, diagonal, 1.0)
                gx_, gy_ = AX[c] * g, AY[c] * g
                q = -fric[t] * vel[c][t]
                co[CE + c, t, at, :] = gx_ * east
                co[CW + c, t, at, :] = gx_ * west
                co[CN + c, t, at, :] = gy_ * north
                co[CS + c, t, at, :] = gy_ * south
                co[SB + c, t, at, :] = g * q
                co[GM + c, t, at, :] = g * misfit[t]
                co[CQ + c, t, at, :] = q
        return 0

    lax.fori_loop(0, blocks // 2, lambda i, x: [coefficients(2 * i + j, x) for j in range(2)][0], 0)
    unpack(1)

    def coef(p, t, r):
        return jnp.broadcast_to(co[p, t, pl.ds(r, 1), :], (8, 128))

    def first_level(r):
        for t in range(3):
            d = (dr[t, pl.ds(r, 8, stride=full), :] if t < 2 else drc[pl.ds(r, 8, stride=full), :])
            for c in range(2):
                w[0, r, 3 * c + t] = coef(SB + c, t, r) * d

    def level_rows(level, r0, count):
        local = (level - 1) % (SWEEPS - 1) + 1
        src = 0 if local == 1 else 1 + local % 2
        dst = 1 + (local + 1) % 2
        last = level == LEVELS
        half = local == SWEEPS - 1 and not last
        tiles = range(2) if last else range(3)
        sums = [[None, None] for _ in range(count)]
        for c in range(2):
            state = [[w[src, r0 + j, 3 * c + t] for t in range(3)] for j in range(-1, count + 1)]
            for j in range(count):
                r = r0 + j
                up, here, down = state[j], state[j + 1], state[j + 2]
                before, after = around(here)
                for t in tiles:
                    new = 0.2 * here[t] + w[0, r, 3 * c + t]
                    new = new + coef(CE + c, t, r) * down[t] + coef(CW + c, t, r) * up[t]
                    new = new + (coef(CN + c, t, r) * after[t] + coef(CS + c, t, r) * before[t])
                    if last:
                        term = coef(CQ + c, t, r) * new
                        sums[j][t] = term if c == 0 else sums[j][t] + term
                    elif half:
                        w[0, r, 3 * c + t] = coef(GM + c, t, r) * new
                    else:
                        w[dst, r, 3 * c + t] = new
        if last:
            for j in range(count):
                for t in range(2):
                    sk[r0 + j - HR, t] = sums[j][t]

    def a2a_copy(c, o):
        peer = lax.rem(me + o, nd)
        return pltpu.make_async_remote_copy(
            src_ref=sk.at[pl.ds(c * chunk + peer * quarter, quarter)],
            dst_ref=rx.at[me, pl.ds(c * quarter, quarter)],
            send_sem=a2a_send.at[c, o],
            recv_sem=a2a_recv.at[c, o],
            device_id={"dir": peer},
            device_id_type=MESH,
        )

    def own_copy(c):
        return pltpu.make_async_copy(
            sk.at[pl.ds(c * chunk + me * quarter, quarter)],
            rx.at[me, pl.ds(c * quarter, quarter)],
            own_sem.at[c],
        )

    base = HR + LEVELS

    def do_chunk(c, _):
        first = 1 - (c + CHUNKS) // (CHUNKS + 1)
        for level in range(LEVELS + 1):
            stop = base - level + chunk * c
            early = -(-2 * (LEVELS - level) // STEP) * STEP
            lo = stop - chunk + first * (chunk - early)

            def step(i, _):
                if level == 0:
                    for j in range(STEP):
                        first_level(lo + STEP * i + j)
                else:
                    level_rows(level, lo + STEP * i, STEP)
                return 0

            lax.fori_loop(0, (stop - lo) // STEP, step, 0)

        @pl.when(c > 0)
        def _():
            for o in range(1, nd):
                a2a_copy(c - 1, o).start()
            own_copy(c - 1).start()

        return 0

    lax.fori_loop(0, CHUNKS + 1, do_chunk, 0)

    def gathered(c):
        parts = []
        for i in range(quarter):
            for t in range(2):
                x = [rx[g, c * quarter + i, t] for g in range(nd)]
                parts.append(jnp.concatenate(split(jnp.concatenate(x, axis=0)), axis=0))
        return jnp.concatenate(parts, axis=1)

    def gram_chunk(c, acc):
        for o in range(1, nd):
            a2a_copy(c, o).wait_recv()
        own_copy(c).wait()

        both = gathered(c)
        return acc + dot(both, both, (1, 1))

    acc = lax.fori_loop(0, CHUNKS, gram_chunk, jnp.zeros((2 * kk, 2 * kk), F32))
    acc = acc[:kk] + acc[kk:]
    gram = acc[:, :kk] + acc[:, kk:]
    gram = jnp.concatenate([gram, jnp.zeros((kk, 128 - kk), F32)], axis=1)

    def reduce_copy(s, axis, index, count, o):
        return pltpu.make_async_remote_copy(
            src_ref=gs.at[s],
            dst_ref=gr.at[s, index],
            send_sem=ar_send.at[s, o],
            recv_sem=ar_recv.at[s, o],
            device_id={axis: lax.rem(index + o, count)},
            device_id_type=MESH,
        )

    for s, (axis, index, count) in enumerate((("dir", me, nd), ("gy", gy, gy_n), ("gx", gx, gx_n))):
        gs[s] = gram
        gr[s, index] = gram
        for o in range(1, count):
            reduce_copy(s, axis, index, count, o).start()
        for o in range(1, count):
            reduce_copy(s, axis, index, count, o).wait_recv()
        gram = gr[s, 0]
        for j in range(1, count):
            gram = gram + gr[s, j]
    gram = gram / jnp.float32(total)

    line = lax.broadcasted_iota(jnp.int32, (kk, 128), 0)
    place = lax.broadcasted_iota(jnp.int32, (kk, 128), 1)
    m = jnp.where(place == line + kk, 1.0, gram)
    for k in range(kk - 1):
        column = jnp.broadcast_to(m[:, k : k + 1], (kk, 128))
        row = jnp.broadcast_to(m[k : k + 1, :], (kk, 128))
        pivot = jnp.broadcast_to(column[k : k + 1, :], (kk, 128))
        m = m - jnp.where(line > k, column, 0.0) * (row / pivot)
    diag = jnp.sum(jnp.where(place == line, m, 0.0), axis=1, keepdims=True)
    m = m * lax.rsqrt(diag)
    upper_ref[...] = jnp.where(place >= line, m, 0.0)[:, :kk]
    inverse = m[:, kk : 2 * kk]
    inv_hi, inv_lo = split(inverse)
    left = jnp.concatenate(
        [jnp.concatenate([inv_hi, inv_hi], axis=1), jnp.concatenate([inv_lo, inv_lo], axis=1)], axis=0
    )

    def ret_copy(c, o, t):
        peer = lax.rem(me + o, nd)
        return pltpu.make_async_remote_copy(
            src_ref=ob.at[peer, c, t],
            dst_ref=out_hbm.at[:, pl.ds(c * chunk + me * quarter, quarter), pl.ds(128 * t, 128)],
            send_sem=ret_send.at[c, o, t],
            recv_sem=ret_recv.at[c, o, t],
            device_id={"dir": peer},
            device_id_type=MESH,
        )

    def ret_own_copy(c, t):
        return pltpu.make_async_copy(
            ob.at[me, c, t],
            out_hbm.at[:, pl.ds(c * chunk + me * quarter, quarter), pl.ds(128 * t, 128)],
            ret_own.at[c, t],
        )

    def basis_chunk(c, _):
        whole = dot(left, gathered(c), (1, 0))
        whole = whole[:kk] + whole[kk:]
        for i in range(quarter):
            for t in range(2):
                out = whole[:, 128 * (2 * i + t) : 128 * (2 * i + t + 1)]
                for g in range(nd):
                    flat = ob.at[g, c, t].reshape(8 * quarter, 128)
                    flat[pl.ds(i, 8, stride=quarter), :] = out[8 * g : 8 * g + 8]
        for t in range(2):
            for o in range(1, nd):
                ret_copy(c, o, t).start()
            ret_own_copy(c, t).start()
        return 0

    lax.fori_loop(0, CHUNKS, basis_chunk, 0)

    for kind in range(2):

        @pl.when(has_up)
        def _():
            row_copy(kind, True).wait_send()

        @pl.when(has_down)
        def _():
            row_copy(kind, False).wait_send()

        @pl.when(has_left)
        def _():
            col_copy(kind, True).wait_send()

        @pl.when(has_right)
        def _():
            col_copy(kind, False).wait_send()

    for s, (axis, index, count) in enumerate((("dir", me, nd), ("gy", gy, gy_n), ("gx", gx, gx_n))):
        for o in range(1, count):
            reduce_copy(s, axis, index, count, o).wait_send()

    def finish(c, _):
        for o in range(1, nd):
            a2a_copy(c, o).wait_send()
            for t in range(2):
                ret_copy(c, o, t).wait_send()
                ret_copy(c, o, t).wait_recv()
        for t in range(2):
            ret_own_copy(c, t).wait()
        return 0

    lax.fori_loop(0, CHUNKS, finish, 0)


def on_device(mesh, directions, velocity, viscosity, basal_drag, misfit_weight, ice_mask, grounded):
    gx_n, gy_n, nd = (mesh.shape[a] for a in ("gx", "gy", "dir"))
    own, rows, cols = directions.shape
    full = rows + 2 * HR
    chunk = rows // CHUNKS
    quarter = chunk // nd
    kk = own * nd
    total = rows * cols * gx_n * gy_n
    most = max(gx_n, gy_n, nd)
    any_space = pl.BlockSpec(memory_space=pl.ANY)
    dma = pltpu.SemaphoreType.DMA
    vmem = pltpu.VMEM
    return pl.pallas_call(
        functools.partial(kernel, (gx_n, gy_n, nd, rows, total)),
        out_shape=(
            jax.ShapeDtypeStruct((own, rows, cols), F32),
            jax.ShapeDtypeStruct((kk, kk), F32),
        ),
        in_specs=[any_space] * 7,
        out_specs=(any_space, pl.BlockSpec(memory_space=pltpu.VMEM)),
        scratch_shapes=[
            vmem((6, 2, full, 128), F32),
            vmem((6, full, 128), F32),
            vmem((2, 8 * full, 128), F32),
            vmem((8 * full, 128), F32),
            vmem((2, rows, 128), F32),
            vmem((2, 2, rows, 128), jnp.int32),
            vmem((2, 2, full, 128), F32),
            vmem((2, 2, full, 128), F32),
            vmem((14, 3, full, 128), F32),
            vmem((3, full, 6, 8, 128), F32),
            vmem((rows, 2, 8, 128), F32),
            vmem((nd, rows // nd, 2, 8, 128), F32),
            vmem((3, kk, 128), F32),
            vmem((3, most, kk, 128), F32),
            vmem((nd, CHUNKS, 2, 8, quarter, 128), F32),
            dma((14,)),
            dma((2, 2)),
            dma((2, 2)),
            dma((2, 2)),
            dma((2, 2)),
            dma((CHUNKS, nd)),
            dma((CHUNKS, nd)),
            dma((CHUNKS,)),
            dma((3, most)),
            dma((3, most)),
            dma((CHUNKS, nd, 2)),
            dma((CHUNKS, nd, 2)),
            dma((CHUNKS, 2)),
        ],
        compiler_params=pltpu.CompilerParams(
            collective_id=0, has_side_effects=True, vmem_limit_bytes=62 << 20
        ),
        name="sketch",
    )(directions, velocity, viscosity, basal_drag, misfit_weight, ice_mask, grounded)


def solution(mesh):
    placed = (P("dir", "gx", "gy"), P(None, "gx", "gy")) + (P("gx", "gy"),) * 5
    return jax.shard_map(
        functools.partial(on_device, mesh),
        mesh=mesh,
        in_specs=placed,
        out_specs=(P("dir", "gx", "gy"), P()),
        check_vma=False,
    )
```

```python
import functools

import jax
import jax.numpy as jnp
from jax import lax
from jax.experimental import pallas as pl
from jax.experimental.pallas import tpu as pltpu
from jax.sharding import PartitionSpec as P

SWEEPS = 6
DAMPING = 0.8
HR = 16
HC = 16
AX = (4.0, 1.0)
AY = (1.0, 4.0)
LEVELS = 2 * (SWEEPS - 1)
CHUNKS = 4
MESH = pl.DeviceIdType.MESH
F32 = jnp.float32
BF16 = jnp.bfloat16
VEL, VISC, FRIC, MISFIT, KEEP = 0, 2, 3, 4, 5
CE, CW, CN, CS, SB, GM, CQ = range(0, 14, 2)


def split(x):
    hi = x.astype(BF16)
    lo = (x - hi.astype(F32)).astype(BF16)
    return hi, lo


def dot(a, b, contract):
    return lax.dot_general(a, b, ((contract[:1], contract[1:]), ((), ())), preferred_element_type=F32)


def kernel(
    sizes,
    dirs_hbm,
    vel_hbm,
    visc_hbm,
    drag_hbm,
    misfit_hbm,
    mask_hbm,
    ground_hbm,
    out_hbm,
    upper_ref,
    fld,
    dr,
    fldp,
    drp,
    halves,
    spread,
    gather,
    terms,
    raw,
    rawi,
    pks,
    pkr,
    co,
    w,
    sk,
    rx,
    gs,
    gr,
    ob,
    in_sem,
    row_send,
    row_recv,
    col_send,
    col_recv,
    a2a_send,
    a2a_recv,
    own_sem,
    ar_send,
    ar_recv,
    ret_send,
    ret_recv,
    ret_own,
):
    gx_n, gy_n, nd, rows, total = sizes
    full = rows + 2 * HR
    blocks = full // 8
    chunk = rows // CHUNKS
    quarter = chunk // nd
    kk = 8 * nd
    gx, gy, me = (lax.axis_index(a) for a in ("gx", "gy", "dir"))
    lane = lax.broadcasted_iota(jnp.int32, (8, 128), 1)

    barrier = pltpu.get_barrier_semaphore()
    peers = 0
    for axis, index, count in (("gx", gx, gx_n), ("gy", gy, gy_n), ("dir", me, nd)):
        for o in range(1, count):
            pl.semaphore_signal(
                barrier, inc=1, device_id={axis: lax.rem(index + o, count)}, device_id_type=MESH
            )
            peers += 1

    dr4 = dr.reshape(2, 8, full, 128)
    body = pl.ds(HR, rows)
    loads = []
    for t in range(2):
        cols = pl.ds(128 * t, 128)
        loads += [
            (vel_hbm.at[:, :, cols], fld.at[0:2, t, body, :]),
            (visc_hbm.at[:, cols], fld.at[VISC, t, body, :]),
            (misfit_hbm.at[:, cols], fld.at[MISFIT, t, body, :]),
            (drag_hbm.at[:, cols], raw.at[t]),
            (mask_hbm.at[:, cols], rawi.at[0, t]),
            (ground_hbm.at[:, cols], rawi.at[1, t]),
            (dirs_hbm.at[:, :, cols], dr4.at[t, :, body, :]),
        ]
    copies = [pltpu.make_async_copy(s, d, in_sem.at[i]) for i, (s, d) in enumerate(loads)]
    for c in copies:
        c.start()

    def zero_rows(start):
        z = jnp.zeros((HR, 128), F32)
        for t in range(2):
            for p in range(6):
                fld[p, t, pl.ds(start, HR), :] = z
            for k in range(8):
                dr[t, pl.ds(k * full + start, HR), :] = z

    @pl.when(gx == 0)
    def _():
        zero_rows(0)

    @pl.when(gx == gx_n - 1)
    def _():
        zero_rows(HR + rows)

    @pl.when(gy == 0)
    def _():
        pkr[:, 0] = jnp.zeros((2, full, 128), F32)

    @pl.when(gy == gy_n - 1)
    def _():
        pkr[:, 1] = jnp.zeros((2, full, 128), F32)

    cols = 256
    k_in = lax.broadcasted_iota(jnp.int32, (384, 384), 0)
    k_out = lax.broadcasted_iota(jnp.int32, (384, 384), 1)
    inside = jnp.where(k_in < cols + HC, k_in + HC, jnp.where(k_in >= 384 - HC, k_in - (384 - HC), -1))
    third = (k_out % 128) * 3 + k_out // 128
    there = jnp.where(inside == third, 1.0, 0.0).astype(BF16)
    spread[0:384] = there
    spread[384:768] = there
    k_in = lax.broadcasted_iota(jnp.int32, (384, cols), 0)
    k_out = lax.broadcasted_iota(jnp.int32, (384, cols), 1)
    back = jnp.where((k_in % 128) * 3 + k_in // 128 == k_out + HC, 1.0, 0.0).astype(BF16)
    gather[0:384] = back
    gather[384:768] = back

    for c in copies:
        c.wait()
    for t in range(2):
        fld[FRIC, t, body, :] = raw[t] * rawi[1, t].astype(F32)
        fld[KEEP, t, body, :] = rawi[0, t].astype(F32)
    pl.semaphore_wait(barrier, peers)

    top, bottom = pl.ds(HR, HR), pl.ds(rows, HR)
    above, below = pl.ds(0, HR), pl.ds(HR + rows, HR)

    def row_copy(kind, up):
        src, dst = (top, below) if up else (bottom, above)
        ref = (fld, dr4)[kind]
        peer = lax.rem(gx + (gx_n - 1 if up else 1), gx_n)
        return pltpu.make_async_remote_copy(
            src_ref=ref.at[:, :, src, :],
            dst_ref=ref.at[:, :, dst, :],
            send_sem=row_send.at[kind, int(up)],
            recv_sem=row_recv.at[kind, int(up)],
            device_id={"gx": peer},
            device_id_type=MESH,
        )

    has_up, has_down = gx > 0, gx < gx_n - 1
    for kind in range(2):

        @pl.when(has_up)
        def _():
            row_copy(kind, True).start()

        @pl.when(has_down)
        def _():
            row_copy(kind, False).start()

    def col_copy(kind, left):
        peer = lax.rem(gy + (gy_n - 1 if left else 1), gy_n)
        return pltpu.make_async_remote_copy(
            src_ref=pks.at[kind, 0 if left else 1],
            dst_ref=pkr.at[kind, 1 if left else 0],
            send_sem=col_send.at[kind, int(left)],
            recv_sem=col_recv.at[kind, int(left)],
            device_id={"gy": peer},
            device_id_type=MESH,
        )

    has_left, has_right = gy > 0, gy < gy_n - 1

    def plane(kind, p, t, at):
        if kind == 0:
            return fld[p, t, at, :]
        return dr[t, pl.ds(pl.multiple_of(p * full + at.start, 8), 8), :]

    for kind in range(2):
        count = (6, 8)[kind]

        @pl.when(has_down)
        def _():
            row_copy(kind, True).wait_recv()

        @pl.when(has_up)
        def _():
            row_copy(kind, False).wait_recv()

        def pack(i, _):
            at = pl.ds(pl.multiple_of(8 * i, 8), 8)
            to_left = jnp.zeros((8, 128), F32)
            to_right = jnp.zeros((8, 128), F32)
            for p in range(count):
                here = (lane >= HC * p) & (lane < HC * (p + 1))
                first = plane(kind, p, 0, at)
                last = plane(kind, p, 1, at)
                if p:
                    first = pltpu.roll(first, HC * p, axis=1)
                if p != 7:
                    last = pltpu.roll(last, (HC * p - (128 - HC)) % 128, axis=1)
                to_left = jnp.where(here, first, to_left)
                to_right = jnp.where(here, last, to_right)
            pks[kind, 0, at, :] = to_left
            pks[kind, 1, at, :] = to_right
            return 0

        lax.fori_loop(0, blocks // 4, lambda i, x: [pack(4 * i + j, x) for j in range(4)][0], 0)

        @pl.when(has_left)
        def _():
            col_copy(kind, True).start()

        @pl.when(has_right)
        def _():
            col_copy(kind, False).start()

    def unpack(kind):
        count = (6, 8)[kind]

        @pl.when(has_right)
        def _():
            col_copy(kind, True).wait_recv()

        @pl.when(has_left)
        def _():
            col_copy(kind, False).wait_recv()

        def one(i, _):
            at = pl.ds(pl.multiple_of(16 * i, 16), 16)
            left = pkr[kind, 0, at, :]
            right = pkr[kind, 1, at, :]
            lane2 = lax.broadcasted_iota(jnp.int32, (16, 128), 1)
            for p in range(count):
                r = right if p == 0 else pltpu.roll(right, 128 - HC * p, axis=1)
                l = left if p == 7 else pltpu.roll(left, 128 - HC * (p + 1), axis=1)
                edge = jnp.where(lane2 < HC, r, jnp.where(lane2 >= 128 - HC, l, 0.0))
                if kind == 0:
                    whole = [fld[p, 0, at, :], fld[p, 1, at, :], edge]
                else:
                    own = pl.ds(pl.multiple_of(p * full + 16 * i, 16), 16)
                    whole = [dr[0, own, :], dr[1, own, :], edge]
                rows_at = pl.ds(pl.multiple_of((6 * kind + p) * full + 16 * i, 16), 16)
                for t in range(3):
                    hi, lo = split(whole[t])
                    halves[rows_at, 128 * t : 128 * t + 128] = hi
                    halves[rows_at, 384 + 128 * t : 512 + 128 * t] = lo
            return 0

        lax.fori_loop(0, full // 32, lambda i, x: [one(2 * i + j, x) for j in range(2)][0], 0)
        size = 2 * full

        def spread_out(i, _):
            part = halves[pl.ds(pl.multiple_of(6 * kind * full + i * size, 16), size), :]
            out = dot(part, spread[...], (1, 0))
            for t in range(3):
                ref = (fldp, drp)[kind]
                ref[t, pl.ds(pl.multiple_of(i * size, 8), size), :] = out[:, 128 * t : 128 * t + 128]
            return 0

        lax.fori_loop(0, count // 2, spread_out, 0)

    unpack(0)

    def around(tiles):
        before = [pltpu.roll(tiles[2], 1, axis=1), tiles[0], tiles[1]]
        after = [tiles[1], tiles[2], pltpu.roll(tiles[0], 127, axis=1)]
        return before, after

    def coefficients(i, _):
        at = pl.ds(pl.multiple_of(8 * i, 8), 8)
        this = 8 * i
        prev_at = 8 * lax.rem(i + blocks - 1, blocks)
        next_at = 8 * lax.rem(i + 1, blocks)

        def field(p, start):
            return [fldp[t, pl.ds(pl.multiple_of(p * full + start, 8), 8), :] for t in range(3)]

        sub = lax.broadcasted_iota(jnp.int32, (8, 128), 0)
        visc = field(VISC, this)
        up, down = field(VISC, prev_at), field(VISC, next_at)
        before, after = around(visc)
        fric, misfit, keep = field(FRIC, this), field(MISFIT, this), field(KEEP, this)
        vel = [field(VEL, this), field(VEL + 1, this)]
        for t in range(3):
            v = visc[t]
            below_row = jnp.where(sub == 7, pltpu.roll(down[t], 7, axis=0), pltpu.roll(v, 7, axis=0))
            above_row = jnp.where(sub == 0, pltpu.roll(up[t], 1, axis=0), pltpu.roll(v, 1, axis=0))
            east, west = 0.5 * (v + below_row), 0.5 * (v + above_row)
            north, south = 0.5 * (v + after[t]), 0.5 * (v + before[t])
            for c in range(2):
                diagonal = AX[c] * (east + west) + AY[c] * (north + south) + fric[t]
                g = (DAMPING * keep[t]) / jnp.where(keep[t] > 0.0, diagonal, 1.0)
                gx_, gy_ = AX[c] * g, AY[c] * g
                q = -fric[t] * vel[c][t]
                co[CE + c, t, at, :] = gx_ * east
                co[CW + c, t, at, :] = gx_ * west
                co[CN + c, t, at, :] = gy_ * north
                co[CS + c, t, at, :] = gy_ * south
                co[SB + c, t, at, :] = g * q
                co[GM + c, t, at, :] = g * misfit[t]
                co[CQ + c, t, at, :] = q
        return 0

    lax.fori_loop(0, blocks // 2, lambda i, x: [coefficients(2 * i + j, x) for j in range(2)][0], 0)
    unpack(1)

    def coef(p, t, r):
        return jnp.broadcast_to(co[p, t, pl.ds(r, 1), :], (8, 128))

    def first_level(r):
        for t in range(3):
            d = drp[t, pl.ds(r, 8, stride=full), :]
            for c in range(2):
                w[0, r, 3 * c + t] = coef(SB + c, t, r) * d

    def level_rows(level, r0, count):
        local = (level - 1) % (SWEEPS - 1) + 1
        src = 0 if local == 1 else 1 + local % 2
        dst = 1 + (local + 1) % 2
        last = level == LEVELS
        half = local == SWEEPS - 1 and not last
        tiles = range(3)
        sums = [[None] * 3 for _ in range(count)]
        for c in range(2):
            state = [[w[src, r0 + j, 3 * c + t] for t in range(3)] for j in range(-1, count + 1)]
            for j in range(count):
                r = r0 + j
                up, here, down = state[j], state[j + 1], state[j + 2]
                before, after = around(here)
                for t in tiles:
                    new = 0.2 * here[t] + w[0, r, 3 * c + t]
                    new = new + coef(CE + c, t, r) * down[t] + coef(CW + c, t, r) * up[t]
                    new = new + (coef(CN + c, t, r) * after[t] + coef(CS + c, t, r) * before[t])
                    if last:
                        term = coef(CQ + c, t, r) * new
                        sums[j][t] = term if c == 0 else sums[j][t] + term
                    elif half:
                        w[0, r, 3 * c + t] = coef(GM + c, t, r) * new
                    else:
                        w[dst, r, 3 * c + t] = new
        if last:
            for j in range(count):
                for t in range(3):
                    terms[8 * j : 8 * j + 8, 128 * t : 128 * t + 128] = sums[j][t]

    def a2a_copy(c, o):
        peer = lax.rem(me + o, nd)
        return pltpu.make_async_remote_copy(
            src_ref=sk.at[pl.ds(c * chunk + peer * quarter, quarter)],
            dst_ref=rx.at[me, pl.ds(c * quarter, quarter)],
            send_sem=a2a_send.at[c, o],
            recv_sem=a2a_recv.at[c, o],
            device_id={"dir": peer},
            device_id_type=MESH,
        )

    def own_copy(c):
        return pltpu.make_async_copy(
            sk.at[pl.ds(c * chunk + me * quarter, quarter)],
            rx.at[me, pl.ds(c * quarter, quarter)],
            own_sem.at[c],
        )

    def do_level(level, lo, count):
        if level == 0:
            for j in range(count):
                first_level(lo + j)
        else:
            level_rows(level, lo, count)

    for level in range(LEVELS):
        do_level(level, HR - LEVELS + level, 2 * (LEVELS - level))

    def do_chunk(c, _):
        for level in range(LEVELS + 1):
            do_level(level, HR + LEVELS - level + chunk * c, chunk)
        out = dot(jnp.concatenate(split(terms[...]), axis=1), gather[...], (1, 0))
        for i in range(chunk):
            for t in range(2):
                sk[c * chunk + i, t] = out[8 * i : 8 * i + 8, 128 * t : 128 * t + 128]
        for o in range(1, nd):
            a2a_copy(c, o).start()
        own_copy(c).start()
        return 0

    lax.fori_loop(0, CHUNKS, do_chunk, 0)

    def gathered(c):
        parts = []
        for i in range(quarter):
            for t in range(2):
                x = [rx[g, c * quarter + i, t] for g in range(nd)]
                parts.append(jnp.concatenate(split(jnp.concatenate(x, axis=0)), axis=0))
        return jnp.concatenate(parts, axis=1)

    def gram_chunk(c, acc):
        for o in range(1, nd):
            a2a_copy(c, o).wait_recv()
        own_copy(c).wait()

        both = gathered(c)
        return acc + dot(both, both, (1, 1))

    acc = lax.fori_loop(0, CHUNKS, gram_chunk, jnp.zeros((2 * kk, 2 * kk), F32))
    acc = acc[:kk] + acc[kk:]
    gram = acc[:, :kk] + acc[:, kk:]
    gram = jnp.concatenate([gram, jnp.zeros((kk, 128 - kk), F32)], axis=1)

    def reduce_copy(s, axis, index, count, o):
        return pltpu.make_async_remote_copy(
            src_ref=gs.at[s],
            dst_ref=gr.at[s, index],
            send_sem=ar_send.at[s, o],
            recv_sem=ar_recv.at[s, o],
            device_id={axis: lax.rem(index + o, count)},
            device_id_type=MESH,
        )

    for s, (axis, index, count) in enumerate((("dir", me, nd), ("gy", gy, gy_n), ("gx", gx, gx_n))):
        gs[s] = gram
        gr[s, index] = gram
        for o in range(1, count):
            reduce_copy(s, axis, index, count, o).start()
        for o in range(1, count):
            reduce_copy(s, axis, index, count, o).wait_recv()
        gram = gr[s, 0]
        for j in range(1, count):
            gram = gram + gr[s, j]
    gram = gram / jnp.float32(total)

    line = lax.broadcasted_iota(jnp.int32, (kk, 128), 0)
    place = lax.broadcasted_iota(jnp.int32, (kk, 128), 1)
    m = jnp.where(place == line + kk, 1.0, gram)
    for k in range(kk - 1):
        column = jnp.broadcast_to(m[:, k : k + 1], (kk, 128))
        row = jnp.broadcast_to(m[k : k + 1, :], (kk, 128))
        pivot = jnp.broadcast_to(column[k : k + 1, :], (kk, 128))
        m = m - jnp.where(line > k, column, 0.0) * (row / pivot)
    diag = jnp.sum(jnp.where(place == line, m, 0.0), axis=1, keepdims=True)
    m = m * lax.rsqrt(diag)
    upper_ref[...] = jnp.where(place >= line, m, 0.0)[:, :kk]
    inverse = m[:, kk : 2 * kk]
    inv_hi, inv_lo = split(inverse)
    left = jnp.concatenate(
        [jnp.concatenate([inv_hi, inv_hi], axis=1), jnp.concatenate([inv_lo, inv_lo], axis=1)], axis=0
    )

    def ret_copy(c, o, t):
        peer = lax.rem(me + o, nd)
        return pltpu.make_async_remote_copy(
            src_ref=ob.at[peer, c, t],
            dst_ref=out_hbm.at[:, pl.ds(c * chunk + me * quarter, quarter), pl.ds(128 * t, 128)],
            send_sem=ret_send.at[c, o, t],
            recv_sem=ret_recv.at[c, o, t],
            device_id={"dir": peer},
            device_id_type=MESH,
        )

    def ret_own_copy(c, t):
        return pltpu.make_async_copy(
            ob.at[me, c, t],
            out_hbm.at[:, pl.ds(c * chunk + me * quarter, quarter), pl.ds(128 * t, 128)],
            ret_own.at[c, t],
        )

    def basis_chunk(c, _):
        whole = dot(left, gathered(c), (1, 0))
        whole = whole[:kk] + whole[kk:]
        for i in range(quarter):
            for t in range(2):
                out = whole[:, 128 * (2 * i + t) : 128 * (2 * i + t + 1)]
                for g in range(nd):
                    flat = ob.at[g, c, t].reshape(8 * quarter, 128)
                    flat[pl.ds(i, 8, stride=quarter), :] = out[8 * g : 8 * g + 8]
        for t in range(2):
            for o in range(1, nd):
                ret_copy(c, o, t).start()
            ret_own_copy(c, t).start()
        return 0

    lax.fori_loop(0, CHUNKS, basis_chunk, 0)

    for kind in range(2):

        @pl.when(has_up)
        def _():
            row_copy(kind, True).wait_send()

        @pl.when(has_down)
        def _():
            row_copy(kind, False).wait_send()

        @pl.when(has_left)
        def _():
            col_copy(kind, True).wait_send()

        @pl.when(has_right)
        def _():
            col_copy(kind, False).wait_send()

    for s, (axis, index, count) in enumerate((("dir", me, nd), ("gy", gy, gy_n), ("gx", gx, gx_n))):
        for o in range(1, count):
            reduce_copy(s, axis, index, count, o).wait_send()

    def finish(c, _):
        for o in range(1, nd):
            a2a_copy(c, o).wait_send()
            for t in range(2):
                ret_copy(c, o, t).wait_send()
                ret_copy(c, o, t).wait_recv()
        for t in range(2):
            ret_own_copy(c, t).wait()
        return 0

    lax.fori_loop(0, CHUNKS, finish, 0)


def on_device(mesh, directions, velocity, viscosity, basal_drag, misfit_weight, ice_mask, grounded):
    gx_n, gy_n, nd = (mesh.shape[a] for a in ("gx", "gy", "dir"))
    own, rows, cols = directions.shape
    full = rows + 2 * HR
    chunk = rows // CHUNKS
    quarter = chunk // nd
    kk = own * nd
    total = rows * cols * gx_n * gy_n
    most = max(gx_n, gy_n, nd)
    any_space = pl.BlockSpec(memory_space=pl.ANY)
    dma = pltpu.SemaphoreType.DMA
    vmem = pltpu.VMEM
    return pl.pallas_call(
        functools.partial(kernel, (gx_n, gy_n, nd, rows, total)),
        out_shape=(
            jax.ShapeDtypeStruct((own, rows, cols), F32),
            jax.ShapeDtypeStruct((kk, kk), F32),
        ),
        in_specs=[any_space] * 7,
        out_specs=(any_space, pl.BlockSpec(memory_space=pltpu.VMEM)),
        scratch_shapes=[
            vmem((6, 2, full, 128), F32),
            vmem((2, 8 * full, 128), F32),
            vmem((3, 6 * full, 128), F32),
            vmem((3, 8 * full, 128), F32),
            vmem((14 * full, 768), BF16),
            vmem((768, 384), BF16),
            vmem((768, cols), BF16),
            vmem((chunk * own, 384), F32),
            vmem((2, rows, 128), F32),
            vmem((2, 2, rows, 128), jnp.int32),
            vmem((2, 2, full, 128), F32),
            vmem((2, 2, full, 128), F32),
            vmem((14, 3, full, 128), F32),
            vmem((3, full, 6, 8, 128), F32),
            vmem((rows, 2, 8, 128), F32),
            vmem((nd, rows // nd, 2, 8, 128), F32),
            vmem((3, kk, 128), F32),
            vmem((3, most, kk, 128), F32),
            vmem((nd, CHUNKS, 2, 8, quarter, 128), F32),
            dma((14,)),
            dma((2, 2)),
            dma((2, 2)),
            dma((2, 2)),
            dma((2, 2)),
            dma((CHUNKS, nd)),
            dma((CHUNKS, nd)),
            dma((CHUNKS,)),
            dma((3, most)),
            dma((3, most)),
            dma((CHUNKS, nd, 2)),
            dma((CHUNKS, nd, 2)),
            dma((CHUNKS, 2)),
        ],
        compiler_params=pltpu.CompilerParams(
            collective_id=0, has_side_effects=True, vmem_limit_bytes=62 << 20
        ),
        name="sketch",
    )(directions, velocity, viscosity, basal_drag, misfit_weight, ice_mask, grounded)


def solution(mesh):
    placed = (P("dir", "gx", "gy"), P(None, "gx", "gy")) + (P("gx", "gy"),) * 5
    return jax.shard_map(
        functools.partial(on_device, mesh),
        mesh=mesh,
        in_specs=placed,
        out_specs=(P("dir", "gx", "gy"), P()),
        check_vma=False,
    )
```

```python
import functools

import jax
import jax.numpy as jnp
from jax import lax
from jax.experimental import pallas as pl
from jax.experimental.pallas import tpu as pltpu
from jax.sharding import PartitionSpec as P

SWEEPS = 6
DAMPING = 0.8
HR = 16
HC = 16
AX = (4.0, 1.0)
AY = (1.0, 4.0)
LEVELS = 2 * (SWEEPS - 1)
CHUNKS = 4
MESH = pl.DeviceIdType.MESH
F32 = jnp.float32
BF16 = jnp.bfloat16
VEL, VISC, FRIC, MISFIT, KEEP = 0, 2, 3, 4, 5
CE, CW, CN, CS, SB, GM, CQ = range(0, 14, 2)


def split(x):
    hi = x.astype(BF16)
    lo = (x - hi.astype(F32)).astype(BF16)
    return hi, lo


def dot(a, b, contract):
    return lax.dot_general(a, b, ((contract[:1], contract[1:]), ((), ())), preferred_element_type=F32)


def kernel(
    sizes,
    dirs_hbm,
    vel_hbm,
    visc_hbm,
    drag_hbm,
    misfit_hbm,
    mask_hbm,
    ground_hbm,
    out_hbm,
    upper_ref,
    fld,
    dr,
    fldp,
    drp,
    halves,
    spread,
    gather,
    terms,
    raw,
    rawi,
    pks,
    pkr,
    co,
    w,
    sk,
    rx,
    gs,
    gr,
    ob,
    in_sem,
    row_send,
    row_recv,
    col_send,
    col_recv,
    corner_send,
    corner_recv,
    a2a_send,
    a2a_recv,
    own_sem,
    ar_send,
    ar_recv,
    ret_send,
    ret_recv,
    ret_own,
):
    gx_n, gy_n, nd, rows, total = sizes
    full = rows + 2 * HR
    blocks = full // 8
    chunk = rows // CHUNKS
    quarter = chunk // nd
    kk = 8 * nd
    gx, gy, me = (lax.axis_index(a) for a in ("gx", "gy", "dir"))
    lane = lax.broadcasted_iota(jnp.int32, (8, 128), 1)

    barrier = pltpu.get_barrier_semaphore()
    peers = 0
    for axis, index, count in (("gx", gx, gx_n), ("gy", gy, gy_n), ("dir", me, nd)):
        for o in range(1, count):
            pl.semaphore_signal(
                barrier, inc=1, device_id={axis: lax.rem(index + o, count)}, device_id_type=MESH
            )
            peers += 1

    corners = [(up, left) for up in (True, False) for left in (True, False)]
    has_up, has_down = gx > 0, gx < gx_n - 1
    has_left, has_right = gy > 0, gy < gy_n - 1

    def corner_id(up, left):
        return {
            "gx": lax.rem(gx + (gx_n - 1 if up else 1), gx_n),
            "gy": lax.rem(gy + (gy_n - 1 if left else 1), gy_n),
        }

    def at_corner(up, left):
        return (has_up if up else has_down) & (has_left if left else has_right)

    for up, left in corners:
        pl.semaphore_signal(barrier, inc=1, device_id=corner_id(up, left), device_id_type=MESH)
        peers += 1

    dr4 = dr.reshape(2, 8, full, 128)
    body = pl.ds(HR, rows)
    loads = []
    for t in range(2):
        cols = pl.ds(128 * t, 128)
        loads += [
            (vel_hbm.at[:, :, cols], fld.at[0:2, t, body, :]),
            (visc_hbm.at[:, cols], fld.at[VISC, t, body, :]),
            (misfit_hbm.at[:, cols], fld.at[MISFIT, t, body, :]),
            (drag_hbm.at[:, cols], raw.at[t]),
            (mask_hbm.at[:, cols], rawi.at[0, t]),
            (ground_hbm.at[:, cols], rawi.at[1, t]),
            (dirs_hbm.at[:, :, cols], dr4.at[t, :, body, :]),
        ]
    copies = [pltpu.make_async_copy(s, d, in_sem.at[i]) for i, (s, d) in enumerate(loads)]
    for c in copies:
        c.start()

    def zero_rows(start):
        z = jnp.zeros((HR, 128), F32)
        pkr[:, :, pl.ds(start, HR), :] = jnp.zeros((2, 2, HR, 128), F32)
        for t in range(2):
            for p in range(6):
                fld[p, t, pl.ds(start, HR), :] = z
            for k in range(8):
                dr[t, pl.ds(k * full + start, HR), :] = z

    @pl.when(gx == 0)
    def _():
        zero_rows(0)

    @pl.when(gx == gx_n - 1)
    def _():
        zero_rows(HR + rows)

    @pl.when(gy == 0)
    def _():
        pkr[:, 0] = jnp.zeros((2, full, 128), F32)

    @pl.when(gy == gy_n - 1)
    def _():
        pkr[:, 1] = jnp.zeros((2, full, 128), F32)

    cols = 256
    k_in = lax.broadcasted_iota(jnp.int32, (384, 384), 0)
    k_out = lax.broadcasted_iota(jnp.int32, (384, 384), 1)
    inside = jnp.where(k_in < cols + HC, k_in + HC, jnp.where(k_in >= 384 - HC, k_in - (384 - HC), -1))
    third = (k_out % 128) * 3 + k_out // 128
    there = jnp.where(inside == third, 1.0, 0.0).astype(BF16)
    spread[0:384] = there
    spread[384:768] = there
    k_in = lax.broadcasted_iota(jnp.int32, (384, cols), 0)
    k_out = lax.broadcasted_iota(jnp.int32, (384, cols), 1)
    back = jnp.where((k_in % 128) * 3 + k_in // 128 == k_out + HC, 1.0, 0.0).astype(BF16)
    gather[0:384] = back
    gather[384:768] = back

    for c in copies:
        c.wait()
    for t in range(2):
        fld[FRIC, t, body, :] = raw[t] * rawi[1, t].astype(F32)
        fld[KEEP, t, body, :] = rawi[0, t].astype(F32)
    pl.semaphore_wait(barrier, peers)

    top, bottom = pl.ds(HR, HR), pl.ds(rows, HR)
    above, below = pl.ds(0, HR), pl.ds(HR + rows, HR)

    def row_copy(kind, up):
        src, dst = (top, below) if up else (bottom, above)
        ref = (fld, dr4)[kind]
        peer = lax.rem(gx + (gx_n - 1 if up else 1), gx_n)
        return pltpu.make_async_remote_copy(
            src_ref=ref.at[:, :, src, :],
            dst_ref=ref.at[:, :, dst, :],
            send_sem=row_send.at[kind, int(up)],
            recv_sem=row_recv.at[kind, int(up)],
            device_id={"gx": peer},
            device_id_type=MESH,
        )

    for kind in range(2):

        @pl.when(has_up)
        def _():
            row_copy(kind, True).start()

        @pl.when(has_down)
        def _():
            row_copy(kind, False).start()

    def col_copy(kind, left):
        peer = lax.rem(gy + (gy_n - 1 if left else 1), gy_n)
        return pltpu.make_async_remote_copy(
            src_ref=pks.at[kind, 0 if left else 1, body],
            dst_ref=pkr.at[kind, 1 if left else 0, body],
            send_sem=col_send.at[kind, int(left)],
            recv_sem=col_recv.at[kind, int(left)],
            device_id={"gy": peer},
            device_id_type=MESH,
        )

    def corner_copy(kind, up, left):
        which = 2 * int(up) + int(left)
        return pltpu.make_async_remote_copy(
            src_ref=pks.at[kind, 0 if left else 1, top if up else bottom],
            dst_ref=pkr.at[kind, 1 if left else 0, below if up else above],
            send_sem=corner_send.at[kind, which],
            recv_sem=corner_recv.at[kind, which],
            device_id=corner_id(up, left),
            device_id_type=MESH,
        )

    def plane(kind, p, t, at):
        if kind == 0:
            return fld[p, t, at, :]
        return dr[t, pl.ds(pl.multiple_of(p * full + at.start, 8), 8), :]

    for kind in range(2):
        count = (6, 8)[kind]

        def pack(i, _):
            at = pl.ds(pl.multiple_of(HR + 8 * i, 8), 8)
            to_left = jnp.zeros((8, 128), F32)
            to_right = jnp.zeros((8, 128), F32)
            for p in range(count):
                here = (lane >= HC * p) & (lane < HC * (p + 1))
                first = plane(kind, p, 0, at)
                last = plane(kind, p, 1, at)
                if p:
                    first = pltpu.roll(first, HC * p, axis=1)
                if p != 7:
                    last = pltpu.roll(last, (HC * p - (128 - HC)) % 128, axis=1)
                to_left = jnp.where(here, first, to_left)
                to_right = jnp.where(here, last, to_right)
            pks[kind, 0, at, :] = to_left
            pks[kind, 1, at, :] = to_right
            return 0

        lax.fori_loop(0, rows // 32, lambda i, x: [pack(4 * i + j, x) for j in range(4)][0], 0)

        @pl.when(has_left)
        def _():
            col_copy(kind, True).start()

        @pl.when(has_right)
        def _():
            col_copy(kind, False).start()

        for up, left in corners:

            @pl.when(at_corner(up, left))
            def _():
                corner_copy(kind, up, left).start()

    def unpack(kind):
        count = (6, 8)[kind]

        @pl.when(has_down)
        def _():
            row_copy(kind, True).wait_recv()

        @pl.when(has_up)
        def _():
            row_copy(kind, False).wait_recv()

        for up, left in corners:

            @pl.when(at_corner(not up, not left))
            def _():
                corner_copy(kind, up, left).wait_recv()

        @pl.when(has_right)
        def _():
            col_copy(kind, True).wait_recv()

        @pl.when(has_left)
        def _():
            col_copy(kind, False).wait_recv()

        def one(i, _):
            at = pl.ds(pl.multiple_of(16 * i, 16), 16)
            left = pkr[kind, 0, at, :]
            right = pkr[kind, 1, at, :]
            lane2 = lax.broadcasted_iota(jnp.int32, (16, 128), 1)
            for p in range(count):
                r = right if p == 0 else pltpu.roll(right, 128 - HC * p, axis=1)
                l = left if p == 7 else pltpu.roll(left, 128 - HC * (p + 1), axis=1)
                edge = jnp.where(lane2 < HC, r, jnp.where(lane2 >= 128 - HC, l, 0.0))
                if kind == 0:
                    whole = [fld[p, 0, at, :], fld[p, 1, at, :], edge]
                else:
                    own = pl.ds(pl.multiple_of(p * full + 16 * i, 16), 16)
                    whole = [dr[0, own, :], dr[1, own, :], edge]
                rows_at = pl.ds(pl.multiple_of((6 * kind + p) * full + 16 * i, 16), 16)
                for t in range(3):
                    hi, lo = split(whole[t])
                    halves[rows_at, 128 * t : 128 * t + 128] = hi
                    halves[rows_at, 384 + 128 * t : 512 + 128 * t] = lo
            return 0

        lax.fori_loop(0, full // 32, lambda i, x: [one(2 * i + j, x) for j in range(2)][0], 0)
        size = 2 * full

        def spread_out(i, _):
            part = halves[pl.ds(pl.multiple_of(6 * kind * full + i * size, 16), size), :]
            out = dot(part, spread[...], (1, 0))
            for t in range(3):
                ref = (fldp, drp)[kind]
                ref[t, pl.ds(pl.multiple_of(i * size, 8), size), :] = out[:, 128 * t : 128 * t + 128]
            return 0

        lax.fori_loop(0, count // 2, spread_out, 0)

    unpack(0)

    def around(tiles):
        before = [pltpu.roll(tiles[2], 1, axis=1), tiles[0], tiles[1]]
        after = [tiles[1], tiles[2], pltpu.roll(tiles[0], 127, axis=1)]
        return before, after

    def coefficients(i, _):
        at = pl.ds(pl.multiple_of(8 * i, 8), 8)
        this = 8 * i
        prev_at = 8 * lax.rem(i + blocks - 1, blocks)
        next_at = 8 * lax.rem(i + 1, blocks)

        def field(p, start):
            return [fldp[t, pl.ds(pl.multiple_of(p * full + start, 8), 8), :] for t in range(3)]

        sub = lax.broadcasted_iota(jnp.int32, (8, 128), 0)
        visc = field(VISC, this)
        up, down = field(VISC, prev_at), field(VISC, next_at)
        before, after = around(visc)
        fric, misfit, keep = field(FRIC, this), field(MISFIT, this), field(KEEP, this)
        vel = [field(VEL, this), field(VEL + 1, this)]
        for t in range(3):
            v = visc[t]
            below_row = jnp.where(sub == 7, pltpu.roll(down[t], 7, axis=0), pltpu.roll(v, 7, axis=0))
            above_row = jnp.where(sub == 0, pltpu.roll(up[t], 1, axis=0), pltpu.roll(v, 1, axis=0))
            east, west = 0.5 * (v + below_row), 0.5 * (v + above_row)
            north, south = 0.5 * (v + after[t]), 0.5 * (v + before[t])
            for c in range(2):
                diagonal = AX[c] * (east + west) + AY[c] * (north + south) + fric[t]
                g = (DAMPING * keep[t]) / jnp.where(keep[t] > 0.0, diagonal, 1.0)
                gx_, gy_ = AX[c] * g, AY[c] * g
                q = -fric[t] * vel[c][t]
                co[CE + c, t, at, :] = gx_ * east
                co[CW + c, t, at, :] = gx_ * west
                co[CN + c, t, at, :] = gy_ * north
                co[CS + c, t, at, :] = gy_ * south
                co[SB + c, t, at, :] = g * q
                co[GM + c, t, at, :] = g * misfit[t]
                co[CQ + c, t, at, :] = q
        return 0

    lax.fori_loop(0, blocks // 2, lambda i, x: [coefficients(2 * i + j, x) for j in range(2)][0], 0)
    unpack(1)

    def coef(p, t, r):
        return jnp.broadcast_to(co[p, t, pl.ds(r, 1), :], (8, 128))

    def first_level(r):
        for t in range(3):
            d = drp[t, pl.ds(r, 8, stride=full), :]
            for c in range(2):
                w[0, r, 3 * c + t] = coef(SB + c, t, r) * d

    def level_rows(level, r0, count):
        local = (level - 1) % (SWEEPS - 1) + 1
        src = 0 if local == 1 else 1 + local % 2
        dst = 1 + (local + 1) % 2
        last = level == LEVELS
        half = local == SWEEPS - 1 and not last
        tiles = range(3)
        sums = [[None] * 3 for _ in range(count)]
        for c in range(2):
            state = [[w[src, r0 + j, 3 * c + t] for t in range(3)] for j in range(-1, count + 1)]
            for j in range(count):
                r = r0 + j
                up, here, down = state[j], state[j + 1], state[j + 2]
                before, after = around(here)
                for t in tiles:
                    new = 0.2 * here[t] + w[0, r, 3 * c + t]
                    new = new + coef(CE + c, t, r) * down[t] + coef(CW + c, t, r) * up[t]
                    new = new + (coef(CN + c, t, r) * after[t] + coef(CS + c, t, r) * before[t])
                    if last:
                        term = coef(CQ + c, t, r) * new
                        sums[j][t] = term if c == 0 else sums[j][t] + term
                    elif half:
                        w[0, r, 3 * c + t] = coef(GM + c, t, r) * new
                    else:
                        w[dst, r, 3 * c + t] = new
        if last:
            for j in range(count):
                for t in range(3):
                    terms[8 * j : 8 * j + 8, 128 * t : 128 * t + 128] = sums[j][t]

    def a2a_copy(c, o):
        peer = lax.rem(me + o, nd)
        return pltpu.make_async_remote_copy(
            src_ref=sk.at[pl.ds(c * chunk + peer * quarter, quarter)],
            dst_ref=rx.at[me, pl.ds(c * quarter, quarter)],
            send_sem=a2a_send.at[c, o],
            recv_sem=a2a_recv.at[c, o],
            device_id={"dir": peer},
            device_id_type=MESH,
        )

    def own_copy(c):
        return pltpu.make_async_copy(
            sk.at[pl.ds(c * chunk + me * quarter, quarter)],
            rx.at[me, pl.ds(c * quarter, quarter)],
            own_sem.at[c],
        )

    def do_level(level, lo, count):
        if level == 0:
            for j in range(count):
                first_level(lo + j)
        else:
            level_rows(level, lo, count)

    for level in range(LEVELS):
        do_level(level, HR - LEVELS + level, 2 * (LEVELS - level))

    def do_chunk(c, _):
        for level in range(LEVELS + 1):
            do_level(level, HR + LEVELS - level + chunk * c, chunk)
        out = dot(jnp.concatenate(split(terms[...]), axis=1), gather[...], (1, 0))
        for i in range(chunk):
            for t in range(2):
                sk[c * chunk + i, t] = out[8 * i : 8 * i + 8, 128 * t : 128 * t + 128]
        for o in range(1, nd):
            a2a_copy(c, o).start()
        own_copy(c).start()
        return 0

    lax.fori_loop(0, CHUNKS, do_chunk, 0)

    def gathered(c):
        parts = []
        for i in range(quarter):
            for t in range(2):
                x = [rx[g, c * quarter + i, t] for g in range(nd)]
                parts.append(jnp.concatenate(split(jnp.concatenate(x, axis=0)), axis=0))
        return jnp.concatenate(parts, axis=1)

    def gram_chunk(c, acc):
        for o in range(1, nd):
            a2a_copy(c, o).wait_recv()
        own_copy(c).wait()

        both = gathered(c)
        return acc + dot(both, both, (1, 1))

    acc = lax.fori_loop(0, CHUNKS, gram_chunk, jnp.zeros((2 * kk, 2 * kk), F32))
    acc = acc[:kk] + acc[kk:]
    gram = acc[:, :kk] + acc[:, kk:]
    gram = jnp.concatenate([gram[8 * g : 8 * g + 8] for g in range(nd)], axis=1)

    def reduce_copy(s, axis, index, count, o):
        return pltpu.make_async_remote_copy(
            src_ref=gs.at[s],
            dst_ref=gr.at[s, index],
            send_sem=ar_send.at[s, o],
            recv_sem=ar_recv.at[s, o],
            device_id={axis: lax.rem(index + o, count)},
            device_id_type=MESH,
        )

    for s, (axis, index, count) in enumerate((("dir", me, nd), ("gy", gy, gy_n), ("gx", gx, gx_n))):
        gs[s] = gram
        gr[s, index] = gram
        for o in range(1, count):
            reduce_copy(s, axis, index, count, o).start()
        for o in range(1, count):
            reduce_copy(s, axis, index, count, o).wait_recv()
        gram = gr[s, 0]
        for j in range(1, count):
            gram = gram + gr[s, j]
    gram = gram / jnp.float32(total)

    line = lax.broadcasted_iota(jnp.int32, (kk, 128), 0)
    place = lax.broadcasted_iota(jnp.int32, (kk, 128), 1)
    gram = [gram] + [pltpu.roll(gram, 128 - kk * g, axis=1) for g in range(1, nd)]
    gram = jnp.where(place < kk, jnp.concatenate(gram, axis=0), 0.0)
    m = jnp.where(place == line + kk, 1.0, gram)

    def wide(row):
        return jnp.broadcast_to(row, (kk, 128))

    for k in range(0, kk, 2):
        col0 = jnp.broadcast_to(m[:, k : k + 1], (kk, 128))
        col1 = jnp.broadcast_to(m[:, k + 1 : k + 2], (kk, 128))
        row0, row1 = wide(m[k : k + 1, :]), wide(m[k + 1 : k + 2, :])
        p00, p10 = wide(col0[k : k + 1, :]), wide(col0[k + 1 : k + 2, :])
        p01, p11 = wide(col1[k : k + 1, :]), wide(col1[k + 1 : k + 2, :])
        inv0 = 1.0 / p00
        row0 = row0 * inv0
        row1 = row1 - p10 * row0
        over = p01 * inv0
        inv1 = 1.0 / (p11 - p10 * over)
        col1 = col1 - col0 * over
        m = m - (
            jnp.where(line > k, col0, 0.0) * row0
            + jnp.where(line > k + 1, col1, 0.0) * (row1 * inv1)
        )
    diag = jnp.sum(jnp.where(place == line, m, 0.0), axis=1, keepdims=True)
    m = m * lax.rsqrt(diag)
    upper_ref[...] = jnp.where(place >= line, m, 0.0)[:, :kk]
    inverse = m[:, kk : 2 * kk]
    inv_hi, inv_lo = split(inverse)
    left = jnp.concatenate(
        [jnp.concatenate([inv_hi, inv_hi], axis=1), jnp.concatenate([inv_lo, inv_lo], axis=1)], axis=0
    )

    def ret_copy(c, o, t):
        peer = lax.rem(me + o, nd)
        return pltpu.make_async_remote_copy(
            src_ref=ob.at[peer, c, t],
            dst_ref=out_hbm.at[:, pl.ds(c * chunk + me * quarter, quarter), pl.ds(128 * t, 128)],
            send_sem=ret_send.at[c, o, t],
            recv_sem=ret_recv.at[c, o, t],
            device_id={"dir": peer},
            device_id_type=MESH,
        )

    def ret_own_copy(c, t):
        return pltpu.make_async_copy(
            ob.at[me, c, t],
            out_hbm.at[:, pl.ds(c * chunk + me * quarter, quarter), pl.ds(128 * t, 128)],
            ret_own.at[c, t],
        )

    def basis_chunk(c, _):
        whole = dot(left, gathered(c), (1, 0))
        whole = whole[:kk] + whole[kk:]
        for i in range(quarter):
            for t in range(2):
                out = whole[:, 128 * (2 * i + t) : 128 * (2 * i + t + 1)]
                for g in range(nd):
                    flat = ob.at[g, c, t].reshape(8 * quarter, 128)
                    flat[pl.ds(i, 8, stride=quarter), :] = out[8 * g : 8 * g + 8]
        for t in range(2):
            for o in range(1, nd):
                ret_copy(c, o, t).start()
            ret_own_copy(c, t).start()
        return 0

    lax.fori_loop(0, CHUNKS, basis_chunk, 0)

    for kind in range(2):

        @pl.when(has_up)
        def _():
            row_copy(kind, True).wait_send()

        @pl.when(has_down)
        def _():
            row_copy(kind, False).wait_send()

        for up, left in corners:

            @pl.when(at_corner(up, left))
            def _():
                corner_copy(kind, up, left).wait_send()

        @pl.when(has_left)
        def _():
            col_copy(kind, True).wait_send()

        @pl.when(has_right)
        def _():
            col_copy(kind, False).wait_send()

    for s, (axis, index, count) in enumerate((("dir", me, nd), ("gy", gy, gy_n), ("gx", gx, gx_n))):
        for o in range(1, count):
            reduce_copy(s, axis, index, count, o).wait_send()

    def finish(c, _):
        for o in range(1, nd):
            a2a_copy(c, o).wait_send()
            for t in range(2):
                ret_copy(c, o, t).wait_send()
                ret_copy(c, o, t).wait_recv()
        for t in range(2):
            ret_own_copy(c, t).wait()
        return 0

    lax.fori_loop(0, CHUNKS, finish, 0)


def on_device(mesh, directions, velocity, viscosity, basal_drag, misfit_weight, ice_mask, grounded):
    gx_n, gy_n, nd = (mesh.shape[a] for a in ("gx", "gy", "dir"))
    own, rows, cols = directions.shape
    full = rows + 2 * HR
    chunk = rows // CHUNKS
    quarter = chunk // nd
    kk = own * nd
    total = rows * cols * gx_n * gy_n
    most = max(gx_n, gy_n, nd)
    any_space = pl.BlockSpec(memory_space=pl.ANY)
    dma = pltpu.SemaphoreType.DMA
    vmem = pltpu.VMEM
    return pl.pallas_call(
        functools.partial(kernel, (gx_n, gy_n, nd, rows, total)),
        out_shape=(
            jax.ShapeDtypeStruct((own, rows, cols), F32),
            jax.ShapeDtypeStruct((kk, kk), F32),
        ),
        in_specs=[any_space] * 7,
        out_specs=(any_space, pl.BlockSpec(memory_space=pltpu.VMEM)),
        scratch_shapes=[
            vmem((6, 2, full, 128), F32),
            vmem((2, 8 * full, 128), F32),
            vmem((3, 6 * full, 128), F32),
            vmem((3, 8 * full, 128), F32),
            vmem((14 * full, 768), BF16),
            vmem((768, 384), BF16),
            vmem((768, cols), BF16),
            vmem((chunk * own, 384), F32),
            vmem((2, rows, 128), F32),
            vmem((2, 2, rows, 128), jnp.int32),
            vmem((2, 2, full, 128), F32),
            vmem((2, 2, full, 128), F32),
            vmem((14, 3, full, 128), F32),
            vmem((3, full, 6, 8, 128), F32),
            vmem((rows, 2, 8, 128), F32),
            vmem((nd, rows // nd, 2, 8, 128), F32),
            vmem((3, 8, kk * nd), F32),
            vmem((3, most, 8, kk * nd), F32),
            vmem((nd, CHUNKS, 2, 8, quarter, 128), F32),
            dma((14,)),
            dma((2, 2)),
            dma((2, 2)),
            dma((2, 2)),
            dma((2, 2)),
            dma((2, 4)),
            dma((2, 4)),
            dma((CHUNKS, nd)),
            dma((CHUNKS, nd)),
            dma((CHUNKS,)),
            dma((3, most)),
            dma((3, most)),
            dma((CHUNKS, nd, 2)),
            dma((CHUNKS, nd, 2)),
            dma((CHUNKS, 2)),
        ],
        compiler_params=pltpu.CompilerParams(
            collective_id=0, has_side_effects=True, vmem_limit_bytes=62 << 20
        ),
        name="sketch",
    )(directions, velocity, viscosity, basal_drag, misfit_weight, ice_mask, grounded)


def solution(mesh):
    placed = (P("dir", "gx", "gy"), P(None, "gx", "gy")) + (P("gx", "gy"),) * 5
    return jax.shard_map(
        functools.partial(on_device, mesh),
        mesh=mesh,
        in_specs=placed,
        out_specs=(P("dir", "gx", "gy"), P()),
        check_vma=False,
    )
```

```python
import functools

import jax
import jax.numpy as jnp
from jax import lax
from jax.experimental import pallas as pl
from jax.experimental.pallas import tpu as pltpu
from jax.sharding import PartitionSpec as P

SWEEPS = 6
DAMPING = 0.8
HR = 16
HC = 16
AX = (4.0, 1.0)
AY = (1.0, 4.0)
LEVELS = 2 * (SWEEPS - 1)
CHUNKS = 4
MESH = pl.DeviceIdType.MESH
F32 = jnp.float32
BF16 = jnp.bfloat16
VEL, VISC, FRIC, MISFIT, KEEP = 0, 2, 3, 4, 5
CE, CW, CN, CS, SB, GM, CQ = range(0, 14, 2)


def split(x):
    hi = x.astype(BF16)
    lo = (x - hi.astype(F32)).astype(BF16)
    return hi, lo


def dot(a, b, contract):
    return lax.dot_general(a, b, ((contract[:1], contract[1:]), ((), ())), preferred_element_type=F32)


def kernel(
    sizes,
    dirs_hbm,
    vel_hbm,
    visc_hbm,
    drag_hbm,
    misfit_hbm,
    mask_hbm,
    ground_hbm,
    out_hbm,
    upper_ref,
    fld,
    dr,
    fldp,
    drp,
    halves,
    spread,
    gather,
    terms,
    raw,
    rawi,
    pks,
    pkr,
    co,
    w,
    sk,
    rx,
    gs,
    gr,
    ob,
    in_sem,
    row_send,
    row_recv,
    col_send,
    col_recv,
    corner_send,
    corner_recv,
    a2a_send,
    a2a_recv,
    own_sem,
    ar_send,
    ar_recv,
    ret_send,
    ret_recv,
    ret_own,
):
    gx_n, gy_n, nd, rows, total = sizes
    full = rows + 2 * HR
    blocks = full // 8
    chunk = rows // CHUNKS
    quarter = chunk // nd
    kk = 8 * nd
    gx, gy, me = (lax.axis_index(a) for a in ("gx", "gy", "dir"))
    lane = lax.broadcasted_iota(jnp.int32, (8, 128), 1)

    barrier = pltpu.get_barrier_semaphore()
    peers = 0
    for axis, index, count in (("gx", gx, gx_n), ("gy", gy, gy_n), ("dir", me, nd)):
        for o in range(1, count):
            pl.semaphore_signal(
                barrier, inc=1, device_id={axis: lax.rem(index + o, count)}, device_id_type=MESH
            )
            peers += 1

    corners = [(up, left) for up in (True, False) for left in (True, False)]
    has_up, has_down = gx > 0, gx < gx_n - 1
    has_left, has_right = gy > 0, gy < gy_n - 1

    def corner_id(up, left):
        return {
            "gx": lax.rem(gx + (gx_n - 1 if up else 1), gx_n),
            "gy": lax.rem(gy + (gy_n - 1 if left else 1), gy_n),
        }

    def at_corner(up, left):
        return (has_up if up else has_down) & (has_left if left else has_right)

    for up, left in corners:
        pl.semaphore_signal(barrier, inc=1, device_id=corner_id(up, left), device_id_type=MESH)
        peers += 1

    dr4 = dr.reshape(2, 8, full, 128)
    body = pl.ds(HR, rows)
    loads = []
    for t in range(2):
        cols = pl.ds(128 * t, 128)
        loads += [
            (vel_hbm.at[:, :, cols], fld.at[0:2, t, body, :]),
            (visc_hbm.at[:, cols], fld.at[VISC, t, body, :]),
            (misfit_hbm.at[:, cols], fld.at[MISFIT, t, body, :]),
            (drag_hbm.at[:, cols], raw.at[t]),
            (mask_hbm.at[:, cols], rawi.at[0, t]),
            (ground_hbm.at[:, cols], rawi.at[1, t]),
            (dirs_hbm.at[:, :, cols], dr4.at[t, :, body, :]),
        ]
    copies = [pltpu.make_async_copy(s, d, in_sem.at[i]) for i, (s, d) in enumerate(loads)]
    for c in copies:
        c.start()

    def zero_rows(start):
        z = jnp.zeros((HR, 128), F32)
        pkr[:, :, pl.ds(start, HR), :] = jnp.zeros((2, 2, HR, 128), F32)
        for t in range(2):
            for p in range(6):
                fld[p, t, pl.ds(start, HR), :] = z
            for k in range(8):
                dr[t, pl.ds(k * full + start, HR), :] = z

    @pl.when(gx == 0)
    def _():
        zero_rows(0)

    @pl.when(gx == gx_n - 1)
    def _():
        zero_rows(HR + rows)

    @pl.when(gy == 0)
    def _():
        pkr[:, 0] = jnp.zeros((2, full, 128), F32)

    @pl.when(gy == gy_n - 1)
    def _():
        pkr[:, 1] = jnp.zeros((2, full, 128), F32)

    cols = 256
    k_in = lax.broadcasted_iota(jnp.int32, (384, 384), 0)
    k_out = lax.broadcasted_iota(jnp.int32, (384, 384), 1)
    inside = jnp.where(k_in < cols + HC, k_in + HC, jnp.where(k_in >= 384 - HC, k_in - (384 - HC), -1))
    third = (k_out % 128) * 3 + k_out // 128
    there = jnp.where(inside == third, 1.0, 0.0).astype(BF16)
    spread[0:384] = there
    spread[384:768] = there
    k_in = lax.broadcasted_iota(jnp.int32, (384, cols), 0)
    k_out = lax.broadcasted_iota(jnp.int32, (384, cols), 1)
    back = jnp.where((k_in % 128) * 3 + k_in // 128 == k_out + HC, 1.0, 0.0).astype(BF16)
    gather[0:384] = back
    gather[384:768] = back

    for c in copies:
        c.wait()
    for t in range(2):
        fld[FRIC, t, body, :] = raw[t] * rawi[1, t].astype(F32)
        fld[KEEP, t, body, :] = rawi[0, t].astype(F32)
    pl.semaphore_wait(barrier, peers)

    top, bottom = pl.ds(HR, HR), pl.ds(rows, HR)
    above, below = pl.ds(0, HR), pl.ds(HR + rows, HR)

    def row_copy(kind, up):
        src, dst = (top, below) if up else (bottom, above)
        ref = (fld, dr4)[kind]
        peer = lax.rem(gx + (gx_n - 1 if up else 1), gx_n)
        return pltpu.make_async_remote_copy(
            src_ref=ref.at[:, :, src, :],
            dst_ref=ref.at[:, :, dst, :],
            send_sem=row_send.at[kind, int(up)],
            recv_sem=row_recv.at[kind, int(up)],
            device_id={"gx": peer},
            device_id_type=MESH,
        )

    def col_copy(kind, left):
        peer = lax.rem(gy + (gy_n - 1 if left else 1), gy_n)
        return pltpu.make_async_remote_copy(
            src_ref=pks.at[kind, 0 if left else 1, body],
            dst_ref=pkr.at[kind, 1 if left else 0, body],
            send_sem=col_send.at[kind, int(left)],
            recv_sem=col_recv.at[kind, int(left)],
            device_id={"gy": peer},
            device_id_type=MESH,
        )

    def corner_copy(kind, up, left):
        which = 2 * int(up) + int(left)
        return pltpu.make_async_remote_copy(
            src_ref=pks.at[kind, 0 if left else 1, top if up else bottom],
            dst_ref=pkr.at[kind, 1 if left else 0, below if up else above],
            send_sem=corner_send.at[kind, which],
            recv_sem=corner_recv.at[kind, which],
            device_id=corner_id(up, left),
            device_id_type=MESH,
        )

    def plane(kind, p, t, at):
        if kind == 0:
            return fld[p, t, at, :]
        return dr[t, pl.ds(pl.multiple_of(p * full + at.start, 8), 8), :]

    for kind in range(2):
        count = (6, 8)[kind]

        @pl.when(has_up)
        def _():
            row_copy(kind, True).start()

        @pl.when(has_down)
        def _():
            row_copy(kind, False).start()

        def pack(i, _):
            at = pl.ds(pl.multiple_of(HR + 8 * i, 8), 8)
            to_left = jnp.zeros((8, 128), F32)
            to_right = jnp.zeros((8, 128), F32)
            for p in range(count):
                here = (lane >= HC * p) & (lane < HC * (p + 1))
                first = plane(kind, p, 0, at)
                last = plane(kind, p, 1, at)
                if p:
                    first = pltpu.roll(first, HC * p, axis=1)
                if p != 7:
                    last = pltpu.roll(last, (HC * p - (128 - HC)) % 128, axis=1)
                to_left = jnp.where(here, first, to_left)
                to_right = jnp.where(here, last, to_right)
            pks[kind, 0, at, :] = to_left
            pks[kind, 1, at, :] = to_right
            return 0

        lax.fori_loop(0, rows // 32, lambda i, x: [pack(4 * i + j, x) for j in range(4)][0], 0)

        @pl.when(has_left)
        def _():
            col_copy(kind, True).start()

        @pl.when(has_right)
        def _():
            col_copy(kind, False).start()

        for up, left in corners:

            @pl.when(at_corner(up, left))
            def _():
                corner_copy(kind, up, left).start()

    def unpack(kind):
        count = (6, 8)[kind]

        @pl.when(has_down)
        def _():
            row_copy(kind, True).wait_recv()

        @pl.when(has_up)
        def _():
            row_copy(kind, False).wait_recv()

        for up, left in corners:

            @pl.when(at_corner(not up, not left))
            def _():
                corner_copy(kind, up, left).wait_recv()

        @pl.when(has_right)
        def _():
            col_copy(kind, True).wait_recv()

        @pl.when(has_left)
        def _():
            col_copy(kind, False).wait_recv()

        def one(i, _):
            at = pl.ds(pl.multiple_of(16 * i, 16), 16)
            left = pkr[kind, 0, at, :]
            right = pkr[kind, 1, at, :]
            lane2 = lax.broadcasted_iota(jnp.int32, (16, 128), 1)
            for p in range(count):
                r = right if p == 0 else pltpu.roll(right, 128 - HC * p, axis=1)
                l = left if p == 7 else pltpu.roll(left, 128 - HC * (p + 1), axis=1)
                edge = jnp.where(lane2 < HC, r, jnp.where(lane2 >= 128 - HC, l, 0.0))
                if kind == 0:
                    whole = [fld[p, 0, at, :], fld[p, 1, at, :], edge]
                else:
                    own = pl.ds(pl.multiple_of(p * full + 16 * i, 16), 16)
                    whole = [dr[0, own, :], dr[1, own, :], edge]
                rows_at = pl.ds(pl.multiple_of((6 * kind + p) * full + 16 * i, 16), 16)
                for t in range(3):
                    hi, lo = split(whole[t])
                    halves[rows_at, 128 * t : 128 * t + 128] = hi
                    halves[rows_at, 384 + 128 * t : 512 + 128 * t] = lo
            return 0

        lax.fori_loop(0, full // 32, lambda i, x: [one(2 * i + j, x) for j in range(2)][0], 0)
        size = 2 * full

        def spread_out(i, _):
            part = halves[pl.ds(pl.multiple_of(6 * kind * full + i * size, 16), size), :]
            out = dot(part, spread[...], (1, 0))
            for t in range(3):
                ref = (fldp, drp)[kind]
                ref[t, pl.ds(pl.multiple_of(i * size, 8), size), :] = out[:, 128 * t : 128 * t + 128]
            return 0

        lax.fori_loop(0, count // 2, spread_out, 0)

    unpack(0)

    def around(tiles):
        before = [pltpu.roll(tiles[2], 1, axis=1), tiles[0], tiles[1]]
        after = [tiles[1], tiles[2], pltpu.roll(tiles[0], 127, axis=1)]
        return before, after

    def coefficients(i, _):
        at = pl.ds(pl.multiple_of(8 * i, 8), 8)
        this = 8 * i
        prev_at = 8 * lax.rem(i + blocks - 1, blocks)
        next_at = 8 * lax.rem(i + 1, blocks)

        def field(p, start):
            return [fldp[t, pl.ds(pl.multiple_of(p * full + start, 8), 8), :] for t in range(3)]

        sub = lax.broadcasted_iota(jnp.int32, (8, 128), 0)
        visc = field(VISC, this)
        up, down = field(VISC, prev_at), field(VISC, next_at)
        before, after = around(visc)
        fric, misfit, keep = field(FRIC, this), field(MISFIT, this), field(KEEP, this)
        vel = [field(VEL, this), field(VEL + 1, this)]
        for t in range(3):
            v = visc[t]
            below_row = jnp.where(sub == 7, pltpu.roll(down[t], 7, axis=0), pltpu.roll(v, 7, axis=0))
            above_row = jnp.where(sub == 0, pltpu.roll(up[t], 1, axis=0), pltpu.roll(v, 1, axis=0))
            east, west = 0.5 * (v + below_row), 0.5 * (v + above_row)
            north, south = 0.5 * (v + after[t]), 0.5 * (v + before[t])
            for c in range(2):
                diagonal = AX[c] * (east + west) + AY[c] * (north + south) + fric[t]
                g = (DAMPING * keep[t]) / jnp.where(keep[t] > 0.0, diagonal, 1.0)
                gx_, gy_ = AX[c] * g, AY[c] * g
                q = -fric[t] * vel[c][t]
                co[CE + c, t, at, :] = gx_ * east
                co[CW + c, t, at, :] = gx_ * west
                co[CN + c, t, at, :] = gy_ * north
                co[CS + c, t, at, :] = gy_ * south
                co[SB + c, t, at, :] = g * q
                co[GM + c, t, at, :] = g * misfit[t]
                co[CQ + c, t, at, :] = q
        return 0

    lax.fori_loop(0, blocks // 2, lambda i, x: [coefficients(2 * i + j, x) for j in range(2)][0], 0)
    unpack(1)

    def coef(p, t, r):
        return jnp.broadcast_to(co[p, t, pl.ds(r, 1), :], (8, 128))

    def first_level(r):
        for t in range(3):
            d = drp[t, pl.ds(r, 8, stride=full), :]
            for c in range(2):
                w[0, r, 3 * c + t] = coef(SB + c, t, r) * d

    def level_rows(level, r0, count):
        local = (level - 1) % (SWEEPS - 1) + 1
        src = 0 if local == 1 else 1 + local % 2
        dst = 1 + (local + 1) % 2
        last = level == LEVELS
        half = local == SWEEPS - 1 and not last
        tiles = range(3)
        sums = [[None] * 3 for _ in range(count)]
        for c in range(2):
            state = [[w[src, r0 + j, 3 * c + t] for t in range(3)] for j in range(-1, count + 1)]
            for j in range(count):
                r = r0 + j
                up, here, down = state[j], state[j + 1], state[j + 2]
                before, after = around(here)
                for t in tiles:
                    new = 0.2 * here[t] + w[0, r, 3 * c + t]
                    new = new + coef(CE + c, t, r) * down[t] + coef(CW + c, t, r) * up[t]
                    new = new + (coef(CN + c, t, r) * after[t] + coef(CS + c, t, r) * before[t])
                    if last:
                        term = coef(CQ + c, t, r) * new
                        sums[j][t] = term if c == 0 else sums[j][t] + term
                    elif half:
                        w[0, r, 3 * c + t] = coef(GM + c, t, r) * new
                    else:
                        w[dst, r, 3 * c + t] = new
        if last:
            for j in range(count):
                for t in range(3):
                    terms[8 * j : 8 * j + 8, 128 * t : 128 * t + 128] = sums[j][t]

    def a2a_copy(c, o):
        peer = lax.rem(me + o, nd)
        return pltpu.make_async_remote_copy(
            src_ref=sk.at[pl.ds(c * chunk + peer * quarter, quarter)],
            dst_ref=rx.at[me, pl.ds(c * quarter, quarter)],
            send_sem=a2a_send.at[c, o],
            recv_sem=a2a_recv.at[c, o],
            device_id={"dir": peer},
            device_id_type=MESH,
        )

    def own_copy(c):
        return pltpu.make_async_copy(
            sk.at[pl.ds(c * chunk + me * quarter, quarter)],
            rx.at[me, pl.ds(c * quarter, quarter)],
            own_sem.at[c],
        )

    def do_level(level, lo, count):
        if level == 0:
            for j in range(count):
                first_level(lo + j)
        else:
            level_rows(level, lo, count)

    for level in range(LEVELS):
        do_level(level, HR - LEVELS + level, 2 * (LEVELS - level))

    def do_chunk(c, _):
        for level in range(LEVELS + 1):
            do_level(level, HR + LEVELS - level + chunk * c, chunk)
        out = dot(jnp.concatenate(split(terms[...]), axis=1), gather[...], (1, 0))
        for i in range(chunk):
            for t in range(2):
                sk[c * chunk + i, t] = out[8 * i : 8 * i + 8, 128 * t : 128 * t + 128]
        for o in range(1, nd):
            a2a_copy(c, o).start()
        own_copy(c).start()
        return 0

    lax.fori_loop(0, CHUNKS, do_chunk, 0)

    def gathered(c):
        parts = []
        for i in range(quarter):
            for t in range(2):
                x = [rx[g, c * quarter + i, t] for g in range(nd)]
                parts.append(jnp.concatenate(split(jnp.concatenate(x, axis=0)), axis=0))
        return jnp.concatenate(parts, axis=1)

    def gram_chunk(c, acc):
        for o in range(1, nd):
            a2a_copy(c, o).wait_recv()
        own_copy(c).wait()

        both = gathered(c)
        return acc + dot(both, both, (1, 1))

    acc = lax.fori_loop(0, CHUNKS, gram_chunk, jnp.zeros((2 * kk, 2 * kk), F32))
    acc = acc[:kk] + acc[kk:]
    gram = acc[:, :kk] + acc[:, kk:]
    gram = jnp.concatenate([gram[8 * g : 8 * g + 8] for g in range(nd)], axis=1)

    def reduce_copy(s, axis, index, count, o):
        return pltpu.make_async_remote_copy(
            src_ref=gs.at[s],
            dst_ref=gr.at[s, index],
            send_sem=ar_send.at[s, o],
            recv_sem=ar_recv.at[s, o],
            device_id={axis: lax.rem(index + o, count)},
            device_id_type=MESH,
        )

    for s, (axis, index, count) in enumerate((("dir", me, nd), ("gy", gy, gy_n), ("gx", gx, gx_n))):
        gs[s] = gram
        gr[s, index] = gram
        for o in range(1, count):
            reduce_copy(s, axis, index, count, o).start()
        for o in range(1, count):
            reduce_copy(s, axis, index, count, o).wait_recv()
        gram = gr[s, 0]
        for j in range(1, count):
            gram = gram + gr[s, j]
    gram = gram / jnp.float32(total)

    line = lax.broadcasted_iota(jnp.int32, (kk, 128), 0)
    place = lax.broadcasted_iota(jnp.int32, (kk, 128), 1)
    gram = [gram] + [pltpu.roll(gram, 128 - kk * g, axis=1) for g in range(1, nd)]
    gram = jnp.where(place < kk, jnp.concatenate(gram, axis=0), 0.0)
    m = jnp.where(place == line + kk, 1.0, gram)

    def wide(row):
        return jnp.broadcast_to(row, (kk, 128))

    for k in range(0, kk, 2):
        col0 = jnp.broadcast_to(m[:, k : k + 1], (kk, 128))
        col1 = jnp.broadcast_to(m[:, k + 1 : k + 2], (kk, 128))
        row0, row1 = wide(m[k : k + 1, :]), wide(m[k + 1 : k + 2, :])
        p00, p10 = wide(col0[k : k + 1, :]), wide(col0[k + 1 : k + 2, :])
        p01, p11 = wide(col1[k : k + 1, :]), wide(col1[k + 1 : k + 2, :])
        inv0 = 1.0 / p00
        row0 = row0 * inv0
        row1 = row1 - p10 * row0
        over = p01 * inv0
        inv1 = 1.0 / (p11 - p10 * over)
        col1 = col1 - col0 * over
        m = m - (
            jnp.where(line > k, col0, 0.0) * row0
            + jnp.where(line > k + 1, col1, 0.0) * (row1 * inv1)
        )
    diag = jnp.sum(jnp.where(place == line, m, 0.0), axis=1, keepdims=True)
    m = m * lax.rsqrt(diag)
    upper_ref[...] = jnp.where(place >= line, m, 0.0)[:, :kk]
    inverse = m[:, kk : 2 * kk]
    inv_hi, inv_lo = split(inverse)
    left = jnp.concatenate(
        [jnp.concatenate([inv_hi, inv_hi], axis=1), jnp.concatenate([inv_lo, inv_lo], axis=1)], axis=0
    )

    def ret_copy(c, o, t):
        peer = lax.rem(me + o, nd)
        return pltpu.make_async_remote_copy(
            src_ref=ob.at[peer, c, t],
            dst_ref=out_hbm.at[:, pl.ds(c * chunk + me * quarter, quarter), pl.ds(128 * t, 128)],
            send_sem=ret_send.at[c, o, t],
            recv_sem=ret_recv.at[c, o, t],
            device_id={"dir": peer},
            device_id_type=MESH,
        )

    def ret_own_copy(c, t):
        return pltpu.make_async_copy(
            ob.at[me, c, t],
            out_hbm.at[:, pl.ds(c * chunk + me * quarter, quarter), pl.ds(128 * t, 128)],
            ret_own.at[c, t],
        )

    def basis_chunk(c, _):
        whole = dot(left, gathered(c), (1, 0))
        whole = whole[:kk] + whole[kk:]
        for i in range(quarter):
            for t in range(2):
                out = whole[:, 128 * (2 * i + t) : 128 * (2 * i + t + 1)]
                for g in range(nd):
                    flat = ob.at[g, c, t].reshape(8 * quarter, 128)
                    flat[pl.ds(i, 8, stride=quarter), :] = out[8 * g : 8 * g + 8]
        for t in range(2):
            for o in range(1, nd):
                ret_copy(c, o, t).start()
            ret_own_copy(c, t).start()
        return 0

    lax.fori_loop(0, CHUNKS, basis_chunk, 0)

    for kind in range(2):

        @pl.when(has_up)
        def _():
            row_copy(kind, True).wait_send()

        @pl.when(has_down)
        def _():
            row_copy(kind, False).wait_send()

        for up, left in corners:

            @pl.when(at_corner(up, left))
            def _():
                corner_copy(kind, up, left).wait_send()

        @pl.when(has_left)
        def _():
            col_copy(kind, True).wait_send()

        @pl.when(has_right)
        def _():
            col_copy(kind, False).wait_send()

    for s, (axis, index, count) in enumerate((("dir", me, nd), ("gy", gy, gy_n), ("gx", gx, gx_n))):
        for o in range(1, count):
            reduce_copy(s, axis, index, count, o).wait_send()

    def finish(c, _):
        for o in range(1, nd):
            a2a_copy(c, o).wait_send()
            for t in range(2):
                ret_copy(c, o, t).wait_send()
                ret_copy(c, o, t).wait_recv()
        for t in range(2):
            ret_own_copy(c, t).wait()
        return 0

    lax.fori_loop(0, CHUNKS, finish, 0)


def hand_over(basis_in, upper_in, basis_out, upper_out, held, held_upper, in_sem, out_sem):
    count = basis_in.shape[0]
    moves = [(basis_in.at[k], held.at[k], basis_out.at[k]) for k in range(count)]
    moves.append((upper_in, held_upper, upper_out))
    takes = [pltpu.make_async_copy(a, h, in_sem.at[i]) for i, (a, h, _) in enumerate(moves)]
    gives = [pltpu.make_async_copy(h, b, out_sem.at[i]) for i, (_, h, b) in enumerate(moves)]
    for c in takes:
        c.start()
    for take, give in zip(takes, gives):
        take.wait()
        give.start()
    for c in gives:
        c.wait()


def on_device(mesh, directions, velocity, viscosity, basal_drag, misfit_weight, ice_mask, grounded):
    gx_n, gy_n, nd = (mesh.shape[a] for a in ("gx", "gy", "dir"))
    own, rows, cols = directions.shape
    full = rows + 2 * HR
    chunk = rows // CHUNKS
    quarter = chunk // nd
    kk = own * nd
    total = rows * cols * gx_n * gy_n
    most = max(gx_n, gy_n, nd)
    any_space = pl.BlockSpec(memory_space=pl.ANY)
    dma = pltpu.SemaphoreType.DMA
    vmem = pltpu.VMEM
    basis, upper = pl.pallas_call(
        functools.partial(kernel, (gx_n, gy_n, nd, rows, total)),
        out_shape=(
            jax.ShapeDtypeStruct((own, rows, cols), F32),
            jax.ShapeDtypeStruct((kk, kk), F32),
        ),
        in_specs=[any_space] * 7,
        out_specs=(any_space, pl.BlockSpec(memory_space=pltpu.VMEM)),
        scratch_shapes=[
            vmem((6, 2, full, 128), F32),
            vmem((2, 8 * full, 128), F32),
            vmem((3, 6 * full, 128), F32),
            vmem((3, 8 * full, 128), F32),
            vmem((14 * full, 768), BF16),
            vmem((768, 384), BF16),
            vmem((768, cols), BF16),
            vmem((chunk * own, 384), F32),
            vmem((2, rows, 128), F32),
            vmem((2, 2, rows, 128), jnp.int32),
            vmem((2, 2, full, 128), F32),
            vmem((2, 2, full, 128), F32),
            vmem((14, 3, full, 128), F32),
            vmem((3, full, 6, 8, 128), F32),
            vmem((rows, 2, 8, 128), F32),
            vmem((nd, rows // nd, 2, 8, 128), F32),
            vmem((3, 8, kk * nd), F32),
            vmem((3, most, 8, kk * nd), F32),
            vmem((nd, CHUNKS, 2, 8, quarter, 128), F32),
            dma((14,)),
            dma((2, 2)),
            dma((2, 2)),
            dma((2, 2)),
            dma((2, 2)),
            dma((2, 4)),
            dma((2, 4)),
            dma((CHUNKS, nd)),
            dma((CHUNKS, nd)),
            dma((CHUNKS,)),
            dma((3, most)),
            dma((3, most)),
            dma((CHUNKS, nd, 2)),
            dma((CHUNKS, nd, 2)),
            dma((CHUNKS, 2)),
        ],
        compiler_params=pltpu.CompilerParams(
            collective_id=0, has_side_effects=True, vmem_limit_bytes=62 << 20
        ),
        name="sketch",
    )(directions, velocity, viscosity, basal_drag, misfit_weight, ice_mask, grounded)
    return pl.pallas_call(
        hand_over,
        out_shape=(
            jax.ShapeDtypeStruct((own, rows, cols), F32),
            jax.ShapeDtypeStruct((kk, kk), F32),
        ),
        in_specs=[any_space] * 2,
        out_specs=(any_space, any_space),
        scratch_shapes=[
            vmem((own, rows, cols), F32),
            vmem((kk, kk), F32),
            dma((own + 1,)),
            dma((own + 1,)),
        ],
        compiler_params=pltpu.CompilerParams(vmem_limit_bytes=62 << 20),
        name="hand_over",
    )(basis, upper)


def solution(mesh):
    placed = (P("dir", "gx", "gy"), P(None, "gx", "gy")) + (P("gx", "gy"),) * 5
    return jax.shard_map(
        functools.partial(on_device, mesh),
        mesh=mesh,
        in_specs=placed,
        out_specs=(P("dir", "gx", "gy"), P()),
        check_vma=False,
    )
```

```python
import functools

import jax
import jax.numpy as jnp
from jax import lax
from jax.experimental import pallas as pl
from jax.experimental.pallas import tpu as pltpu
from jax.sharding import PartitionSpec as P

SWEEPS = 6
DAMPING = 0.8
HR = 16
HC = 16
AX = (4.0, 1.0)
AY = (1.0, 4.0)
LEVELS = 2 * (SWEEPS - 1)
CHUNKS = 4
MESH = pl.DeviceIdType.MESH
F32 = jnp.float32
BF16 = jnp.bfloat16
VEL, VISC, FRIC, MISFIT, KEEP = 0, 2, 3, 4, 5
CE, CW, CN, CS, SB, GM, CQ = range(0, 14, 2)


def split(x):
    hi = x.astype(BF16)
    lo = (x - hi.astype(F32)).astype(BF16)
    return hi, lo


def dot(a, b, contract):
    return lax.dot_general(a, b, ((contract[:1], contract[1:]), ((), ())), preferred_element_type=F32)


def kernel(
    sizes,
    dirs_hbm,
    vel_hbm,
    visc_hbm,
    drag_hbm,
    misfit_hbm,
    mask_hbm,
    ground_hbm,
    out_hbm,
    upper_ref,
    fld,
    dr,
    fldp,
    drp,
    halves,
    spread,
    gather,
    terms,
    raw,
    rawi,
    pks,
    pkr,
    co,
    w,
    sk,
    rx,
    gs,
    gr,
    ob,
    in_sem,
    row_send,
    row_recv,
    col_send,
    col_recv,
    corner_send,
    corner_recv,
    a2a_send,
    a2a_recv,
    own_sem,
    ar_send,
    ar_recv,
    ret_send,
    ret_recv,
    ret_own,
):
    gx_n, gy_n, nd, rows, total = sizes
    full = rows + 2 * HR
    blocks = full // 8
    chunk = rows // CHUNKS
    quarter = chunk // nd
    kk = 8 * nd
    gx, gy, me = (lax.axis_index(a) for a in ("gx", "gy", "dir"))
    lane = lax.broadcasted_iota(jnp.int32, (8, 128), 1)

    barrier = pltpu.get_barrier_semaphore()
    peers = 0
    for axis, index, count in (("gx", gx, gx_n), ("gy", gy, gy_n), ("dir", me, nd)):
        for o in range(1, count):
            pl.semaphore_signal(
                barrier, inc=1, device_id={axis: lax.rem(index + o, count)}, device_id_type=MESH
            )
            peers += 1

    corners = [(up, left) for up in (True, False) for left in (True, False)]
    has_up, has_down = gx > 0, gx < gx_n - 1
    has_left, has_right = gy > 0, gy < gy_n - 1

    def corner_id(up, left):
        return {
            "gx": lax.rem(gx + (gx_n - 1 if up else 1), gx_n),
            "gy": lax.rem(gy + (gy_n - 1 if left else 1), gy_n),
        }

    def at_corner(up, left):
        return (has_up if up else has_down) & (has_left if left else has_right)

    for up, left in corners:
        pl.semaphore_signal(barrier, inc=1, device_id=corner_id(up, left), device_id_type=MESH)
        peers += 1

    dr4 = dr.reshape(2, 8, full, 128)
    body = pl.ds(HR, rows)
    loads = []
    for t in range(2):
        cols = pl.ds(128 * t, 128)
        loads += [
            (vel_hbm.at[:, :, cols], fld.at[0:2, t, body, :]),
            (visc_hbm.at[:, cols], fld.at[VISC, t, body, :]),
            (misfit_hbm.at[:, cols], fld.at[MISFIT, t, body, :]),
            (drag_hbm.at[:, cols], raw.at[t]),
            (mask_hbm.at[:, cols], rawi.at[0, t]),
            (ground_hbm.at[:, cols], rawi.at[1, t]),
            (dirs_hbm.at[:, :, cols], dr4.at[t, :, body, :]),
        ]
    copies = [pltpu.make_async_copy(s, d, in_sem.at[i]) for i, (s, d) in enumerate(loads)]
    for c in copies:
        c.start()

    def zero_rows(start):
        z = jnp.zeros((HR, 128), F32)
        pkr[:, :, pl.ds(start, HR), :] = jnp.zeros((2, 2, HR, 128), F32)
        for t in range(2):
            for p in range(6):
                fld[p, t, pl.ds(start, HR), :] = z
            for k in range(8):
                dr[t, pl.ds(k * full + start, HR), :] = z

    @pl.when(gx == 0)
    def _():
        zero_rows(0)

    @pl.when(gx == gx_n - 1)
    def _():
        zero_rows(HR + rows)

    @pl.when(gy == 0)
    def _():
        pkr[:, 0] = jnp.zeros((2, full, 128), F32)

    @pl.when(gy == gy_n - 1)
    def _():
        pkr[:, 1] = jnp.zeros((2, full, 128), F32)

    for c in copies:
        c.wait()
    for t in range(2):
        fld[FRIC, t, body, :] = raw[t] * rawi[1, t].astype(F32)
        fld[KEEP, t, body, :] = rawi[0, t].astype(F32)
    pl.semaphore_wait(barrier, peers)

    top, bottom = pl.ds(HR, HR), pl.ds(rows, HR)
    above, below = pl.ds(0, HR), pl.ds(HR + rows, HR)

    def row_copy(kind, up):
        src, dst = (top, below) if up else (bottom, above)
        ref = (fld, dr4)[kind]
        peer = lax.rem(gx + (gx_n - 1 if up else 1), gx_n)
        return pltpu.make_async_remote_copy(
            src_ref=ref.at[:, :, src, :],
            dst_ref=ref.at[:, :, dst, :],
            send_sem=row_send.at[kind, int(up)],
            recv_sem=row_recv.at[kind, int(up)],
            device_id={"gx": peer},
            device_id_type=MESH,
        )

    def col_copy(kind, left):
        peer = lax.rem(gy + (gy_n - 1 if left else 1), gy_n)
        return pltpu.make_async_remote_copy(
            src_ref=pks.at[kind, 0 if left else 1, body],
            dst_ref=pkr.at[kind, 1 if left else 0, body],
            send_sem=col_send.at[kind, int(left)],
            recv_sem=col_recv.at[kind, int(left)],
            device_id={"gy": peer},
            device_id_type=MESH,
        )

    def corner_copy(kind, up, left):
        which = 2 * int(up) + int(left)
        return pltpu.make_async_remote_copy(
            src_ref=pks.at[kind, 0 if left else 1, top if up else bottom],
            dst_ref=pkr.at[kind, 1 if left else 0, below if up else above],
            send_sem=corner_send.at[kind, which],
            recv_sem=corner_recv.at[kind, which],
            device_id=corner_id(up, left),
            device_id_type=MESH,
        )

    def plane(kind, p, t, at):
        if kind == 0:
            return fld[p, t, at, :]
        return dr[t, pl.ds(pl.multiple_of(p * full + at.start, 8), 8), :]

    for kind in range(2):
        count = (6, 8)[kind]

        @pl.when(has_up)
        def _():
            row_copy(kind, True).start()

        @pl.when(has_down)
        def _():
            row_copy(kind, False).start()

        def pack(i, _):
            at = pl.ds(pl.multiple_of(HR + 8 * i, 8), 8)
            to_left = jnp.zeros((8, 128), F32)
            to_right = jnp.zeros((8, 128), F32)
            for p in range(count):
                here = (lane >= HC * p) & (lane < HC * (p + 1))
                first = plane(kind, p, 0, at)
                last = plane(kind, p, 1, at)
                if p:
                    first = pltpu.roll(first, HC * p, axis=1)
                if p != 7:
                    last = pltpu.roll(last, (HC * p - (128 - HC)) % 128, axis=1)
                to_left = jnp.where(here, first, to_left)
                to_right = jnp.where(here, last, to_right)
            pks[kind, 0, at, :] = to_left
            pks[kind, 1, at, :] = to_right
            return 0

        lax.fori_loop(0, rows // 32, lambda i, x: [pack(4 * i + j, x) for j in range(4)][0], 0)

        @pl.when(has_left)
        def _():
            col_copy(kind, True).start()

        @pl.when(has_right)
        def _():
            col_copy(kind, False).start()

        for up, left in corners:

            @pl.when(at_corner(up, left))
            def _():
                corner_copy(kind, up, left).start()

    def unpack(kind):
        count = (6, 8)[kind]

        @pl.when(has_down)
        def _():
            row_copy(kind, True).wait_recv()

        @pl.when(has_up)
        def _():
            row_copy(kind, False).wait_recv()

        for up, left in corners:

            @pl.when(at_corner(not up, not left))
            def _():
                corner_copy(kind, up, left).wait_recv()

        @pl.when(has_right)
        def _():
            col_copy(kind, True).wait_recv()

        @pl.when(has_left)
        def _():
            col_copy(kind, False).wait_recv()

        def one(i, _):
            at = pl.ds(pl.multiple_of(16 * i, 16), 16)
            left = pkr[kind, 0, at, :]
            right = pkr[kind, 1, at, :]
            lane2 = lax.broadcasted_iota(jnp.int32, (16, 128), 1)
            for p in range(count):
                r = right if p == 0 else pltpu.roll(right, 128 - HC * p, axis=1)
                l = left if p == 7 else pltpu.roll(left, 128 - HC * (p + 1), axis=1)
                edge = jnp.where(lane2 < HC, r, jnp.where(lane2 >= 128 - HC, l, 0.0))
                if kind == 0:
                    whole = [fld[p, 0, at, :], fld[p, 1, at, :], edge]
                else:
                    own = pl.ds(pl.multiple_of(p * full + 16 * i, 16), 16)
                    whole = [dr[0, own, :], dr[1, own, :], edge]
                rows_at = pl.ds(pl.multiple_of((6 * kind + p) * full + 16 * i, 16), 16)
                for t in range(3):
                    hi, lo = split(whole[t])
                    halves[rows_at, 128 * t : 128 * t + 128] = hi
                    halves[rows_at, 384 + 128 * t : 512 + 128 * t] = lo
            return 0

        lax.fori_loop(0, full // 32, lambda i, x: [one(2 * i + j, x) for j in range(2)][0], 0)
        size = count // 2 * full

        def spread_out(i, _):
            part = halves[pl.ds(pl.multiple_of(6 * kind * full + i * size, 16), size), :]
            out = dot(part, spread[...], (1, 0))
            for t in range(3):
                ref = (fldp, drp)[kind]
                ref[t, pl.ds(pl.multiple_of(i * size, 8), size), :] = out[:, 128 * t : 128 * t + 128]
            return 0

        lax.fori_loop(0, 2, spread_out, 0)

    cols = 256
    k_in = lax.broadcasted_iota(jnp.int32, (384, 384), 0)
    k_out = lax.broadcasted_iota(jnp.int32, (384, 384), 1)
    inside = jnp.where(k_in < cols + HC, k_in + HC, jnp.where(k_in >= 384 - HC, k_in - (384 - HC), -1))
    third = (k_out % 128) * 3 + k_out // 128
    there = jnp.where(inside == third, 1.0, 0.0).astype(BF16)
    spread[0:384] = there
    spread[384:768] = there
    k_in = lax.broadcasted_iota(jnp.int32, (384, cols), 0)
    k_out = lax.broadcasted_iota(jnp.int32, (384, cols), 1)
    back = jnp.where((k_in % 128) * 3 + k_in // 128 == k_out + HC, 1.0, 0.0).astype(BF16)
    gather[0:384] = back
    gather[384:768] = back

    unpack(0)

    def around(tiles):
        before = [pltpu.roll(tiles[2], 1, axis=1), tiles[0], tiles[1]]
        after = [tiles[1], tiles[2], pltpu.roll(tiles[0], 127, axis=1)]
        return before, after

    def coefficients(i, _):
        at = pl.ds(pl.multiple_of(8 * i, 8), 8)
        this = 8 * i
        prev_at = 8 * lax.rem(i + blocks - 1, blocks)
        next_at = 8 * lax.rem(i + 1, blocks)

        def field(p, start):
            return [fldp[t, pl.ds(pl.multiple_of(p * full + start, 8), 8), :] for t in range(3)]

        sub = lax.broadcasted_iota(jnp.int32, (8, 128), 0)
        visc = field(VISC, this)
        up, down = field(VISC, prev_at), field(VISC, next_at)
        before, after = around(visc)
        fric, misfit, keep = field(FRIC, this), field(MISFIT, this), field(KEEP, this)
        vel = [field(VEL, this), field(VEL + 1, this)]
        for t in range(3):
            v = visc[t]
            below_row = jnp.where(sub == 7, pltpu.roll(down[t], 7, axis=0), pltpu.roll(v, 7, axis=0))
            above_row = jnp.where(sub == 0, pltpu.roll(up[t], 1, axis=0), pltpu.roll(v, 1, axis=0))
            east, west = 0.5 * (v + below_row), 0.5 * (v + above_row)
            north, south = 0.5 * (v + after[t]), 0.5 * (v + before[t])
            for c in range(2):
                diagonal = AX[c] * (east + west) + AY[c] * (north + south) + fric[t]
                g = (DAMPING * keep[t]) / jnp.where(keep[t] > 0.0, diagonal, 1.0)
                gx_, gy_ = AX[c] * g, AY[c] * g
                q = -fric[t] * vel[c][t]
                co[CE + c, t, at, :] = gx_ * east
                co[CW + c, t, at, :] = gx_ * west
                co[CN + c, t, at, :] = gy_ * north
                co[CS + c, t, at, :] = gy_ * south
                co[SB + c, t, at, :] = g * q
                co[GM + c, t, at, :] = g * misfit[t]
                co[CQ + c, t, at, :] = q
        return 0

    lax.fori_loop(0, blocks // 2, lambda i, x: [coefficients(2 * i + j, x) for j in range(2)][0], 0)
    unpack(1)

    def coef(p, t, r):
        return jnp.broadcast_to(co[p, t, pl.ds(r, 1), :], (8, 128))

    def first_level(r):
        for t in range(3):
            d = drp[t, pl.ds(r, 8, stride=full), :]
            for c in range(2):
                w[0, r, 3 * c + t] = coef(SB + c, t, r) * d

    def level_rows(level, r0, count):
        local = (level - 1) % (SWEEPS - 1) + 1
        src = 0 if local == 1 else 1 + local % 2
        dst = 1 + (local + 1) % 2
        last = level == LEVELS
        half = local == SWEEPS - 1 and not last
        tiles = range(3)
        sums = [[None] * 3 for _ in range(count)]
        for c in range(2):
            state = [[w[src, r0 + j, 3 * c + t] for t in range(3)] for j in range(-1, count + 1)]
            for j in range(count):
                r = r0 + j
                up, here, down = state[j], state[j + 1], state[j + 2]
                before, after = around(here)
                for t in tiles:
                    new = 0.2 * here[t] + w[0, r, 3 * c + t]
                    new = new + coef(CE + c, t, r) * down[t] + coef(CW + c, t, r) * up[t]
                    new = new + (coef(CN + c, t, r) * after[t] + coef(CS + c, t, r) * before[t])
                    if last:
                        term = coef(CQ + c, t, r) * new
                        sums[j][t] = term if c == 0 else sums[j][t] + term
                    elif half:
                        w[0, r, 3 * c + t] = coef(GM + c, t, r) * new
                    else:
                        w[dst, r, 3 * c + t] = new
        if last:
            for j in range(count):
                for t in range(3):
                    terms[8 * j : 8 * j + 8, 128 * t : 128 * t + 128] = sums[j][t]

    def a2a_copy(c, o):
        peer = lax.rem(me + o, nd)
        return pltpu.make_async_remote_copy(
            src_ref=sk.at[pl.ds(c * chunk + peer * quarter, quarter)],
            dst_ref=rx.at[me, pl.ds(c * quarter, quarter)],
            send_sem=a2a_send.at[c, o],
            recv_sem=a2a_recv.at[c, o],
            device_id={"dir": peer},
            device_id_type=MESH,
        )

    def own_copy(c):
        return pltpu.make_async_copy(
            sk.at[pl.ds(c * chunk + me * quarter, quarter)],
            rx.at[me, pl.ds(c * quarter, quarter)],
            own_sem.at[c],
        )

    def do_level(level, lo, count):
        if level == 0:
            for j in range(count):
                first_level(lo + j)
        else:
            level_rows(level, lo, count)

    for level in range(LEVELS):
        do_level(level, HR - LEVELS + level, 2 * (LEVELS - level))

    def do_chunk(c, _):
        for level in range(LEVELS + 1):
            do_level(level, HR + LEVELS - level + chunk * c, chunk)
        out = dot(jnp.concatenate(split(terms[...]), axis=1), gather[...], (1, 0))
        for i in range(chunk):
            for t in range(2):
                sk[c * chunk + i, t] = out[8 * i : 8 * i + 8, 128 * t : 128 * t + 128]
        for o in range(1, nd):
            a2a_copy(c, o).start()
        own_copy(c).start()
        return 0

    lax.fori_loop(0, CHUNKS, do_chunk, 0)

    def gathered(c):
        parts = []
        for i in range(quarter):
            for t in range(2):
                x = [rx[g, c * quarter + i, t] for g in range(nd)]
                parts.append(jnp.concatenate(split(jnp.concatenate(x, axis=0)), axis=0))
        return jnp.concatenate(parts, axis=1)

    def gram_chunk(c, acc):
        for o in range(1, nd):
            a2a_copy(c, o).wait_recv()
        own_copy(c).wait()

        both = gathered(c)
        return acc + dot(both, both, (1, 1))

    acc = lax.fori_loop(0, CHUNKS, gram_chunk, jnp.zeros((2 * kk, 2 * kk), F32))
    acc = acc[:kk] + acc[kk:]
    gram = acc[:, :kk] + acc[:, kk:]
    gram = jnp.concatenate([gram[8 * g : 8 * g + 8] for g in range(nd)], axis=1)

    def reduce_copy(s, axis, index, count, o):
        return pltpu.make_async_remote_copy(
            src_ref=gs.at[s],
            dst_ref=gr.at[s, index],
            send_sem=ar_send.at[s, o],
            recv_sem=ar_recv.at[s, o],
            device_id={axis: lax.rem(index + o, count)},
            device_id_type=MESH,
        )

    for s, (axis, index, count) in enumerate((("dir", me, nd), ("gy", gy, gy_n), ("gx", gx, gx_n))):
        gs[s] = gram
        gr[s, index] = gram
        for o in range(1, count):
            reduce_copy(s, axis, index, count, o).start()
        for o in range(1, count):
            reduce_copy(s, axis, index, count, o).wait_recv()
        gram = gr[s, 0]
        for j in range(1, count):
            gram = gram + gr[s, j]
    gram = gram / jnp.float32(total)

    line = lax.broadcasted_iota(jnp.int32, (kk, 128), 0)
    place = lax.broadcasted_iota(jnp.int32, (kk, 128), 1)
    gram = [gram] + [pltpu.roll(gram, 128 - kk * g, axis=1) for g in range(1, nd)]
    gram = jnp.where(place < kk, jnp.concatenate(gram, axis=0), 0.0)
    m = jnp.where(place == line + kk, 1.0, gram)

    def wide(row):
        return jnp.broadcast_to(row, (kk, 128))

    for k in range(0, kk, 2):
        col0 = jnp.broadcast_to(m[:, k : k + 1], (kk, 128))
        col1 = jnp.broadcast_to(m[:, k + 1 : k + 2], (kk, 128))
        row0, row1 = wide(m[k : k + 1, :]), wide(m[k + 1 : k + 2, :])
        p00, p10 = wide(col0[k : k + 1, :]), wide(col0[k + 1 : k + 2, :])
        p01, p11 = wide(col1[k : k + 1, :]), wide(col1[k + 1 : k + 2, :])
        inv0 = 1.0 / p00
        row0 = row0 * inv0
        row1 = row1 - p10 * row0
        over = p01 * inv0
        inv1 = 1.0 / (p11 - p10 * over)
        col1 = col1 - col0 * over
        m = m - (
            jnp.where(line > k, col0, 0.0) * row0
            + jnp.where(line > k + 1, col1, 0.0) * (row1 * inv1)
        )
    diag = jnp.sum(jnp.where(place == line, m, 0.0), axis=1, keepdims=True)
    m = m * lax.rsqrt(diag)
    upper_ref[...] = jnp.where(place >= line, m, 0.0)[:, :kk]
    inverse = m[:, kk : 2 * kk]
    inv_hi, inv_lo = split(inverse)
    left = jnp.concatenate(
        [jnp.concatenate([inv_hi, inv_hi], axis=1), jnp.concatenate([inv_lo, inv_lo], axis=1)], axis=0
    )

    def ret_copy(c, o, t):
        peer = lax.rem(me + o, nd)
        return pltpu.make_async_remote_copy(
            src_ref=ob.at[peer, c, t],
            dst_ref=out_hbm.at[:, pl.ds(c * chunk + me * quarter, quarter), pl.ds(128 * t, 128)],
            send_sem=ret_send.at[c, o, t],
            recv_sem=ret_recv.at[c, o, t],
            device_id={"dir": peer},
            device_id_type=MESH,
        )

    def ret_own_copy(c, t):
        return pltpu.make_async_copy(
            ob.at[me, c, t],
            out_hbm.at[:, pl.ds(c * chunk + me * quarter, quarter), pl.ds(128 * t, 128)],
            ret_own.at[c, t],
        )

    def basis_chunk(c, _):
        whole = dot(left, gathered(c), (1, 0))
        whole = whole[:kk] + whole[kk:]
        for i in range(quarter):
            for t in range(2):
                out = whole[:, 128 * (2 * i + t) : 128 * (2 * i + t + 1)]
                for g in range(nd):
                    flat = ob.at[g, c, t].reshape(8 * quarter, 128)
                    flat[pl.ds(i, 8, stride=quarter), :] = out[8 * g : 8 * g + 8]
        for t in range(2):
            for o in range(1, nd):
                ret_copy(c, o, t).start()
            ret_own_copy(c, t).start()
        return 0

    lax.fori_loop(0, CHUNKS, basis_chunk, 0)

    for kind in range(2):

        @pl.when(has_up)
        def _():
            row_copy(kind, True).wait_send()

        @pl.when(has_down)
        def _():
            row_copy(kind, False).wait_send()

        for up, left in corners:

            @pl.when(at_corner(up, left))
            def _():
                corner_copy(kind, up, left).wait_send()

        @pl.when(has_left)
        def _():
            col_copy(kind, True).wait_send()

        @pl.when(has_right)
        def _():
            col_copy(kind, False).wait_send()

    for s, (axis, index, count) in enumerate((("dir", me, nd), ("gy", gy, gy_n), ("gx", gx, gx_n))):
        for o in range(1, count):
            reduce_copy(s, axis, index, count, o).wait_send()

    def finish(c, _):
        for o in range(1, nd):
            a2a_copy(c, o).wait_send()
            for t in range(2):
                ret_copy(c, o, t).wait_send()
                ret_copy(c, o, t).wait_recv()
        for t in range(2):
            ret_own_copy(c, t).wait()
        return 0

    lax.fori_loop(0, CHUNKS, finish, 0)


def hand_over(basis_in, upper_in, basis_out, upper_out, held, held_upper, in_sem, out_sem):
    count = basis_in.shape[0]
    moves = [(basis_in.at[k], held.at[k], basis_out.at[k]) for k in range(count)]
    moves.append((upper_in, held_upper, upper_out))
    takes = [pltpu.make_async_copy(a, h, in_sem.at[i]) for i, (a, h, _) in enumerate(moves)]
    gives = [pltpu.make_async_copy(h, b, out_sem.at[i]) for i, (_, h, b) in enumerate(moves)]
    for c in takes:
        c.start()
    for take, give in zip(takes, gives):
        take.wait()
        give.start()
    for c in gives:
        c.wait()


def on_device(mesh, directions, velocity, viscosity, basal_drag, misfit_weight, ice_mask, grounded):
    gx_n, gy_n, nd = (mesh.shape[a] for a in ("gx", "gy", "dir"))
    own, rows, cols = directions.shape
    full = rows + 2 * HR
    chunk = rows // CHUNKS
    quarter = chunk // nd
    kk = own * nd
    total = rows * cols * gx_n * gy_n
    most = max(gx_n, gy_n, nd)
    any_space = pl.BlockSpec(memory_space=pl.ANY)
    dma = pltpu.SemaphoreType.DMA
    vmem = pltpu.VMEM
    basis, upper = pl.pallas_call(
        functools.partial(kernel, (gx_n, gy_n, nd, rows, total)),
        out_shape=(
            jax.ShapeDtypeStruct((own, rows, cols), F32),
            jax.ShapeDtypeStruct((kk, kk), F32),
        ),
        in_specs=[any_space] * 7,
        out_specs=(any_space, pl.BlockSpec(memory_space=pltpu.VMEM)),
        scratch_shapes=[
            vmem((6, 2, full, 128), F32),
            vmem((2, 8 * full, 128), F32),
            vmem((3, 6 * full, 128), F32),
            vmem((3, 8 * full, 128), F32),
            vmem((14 * full, 768), BF16),
            vmem((768, 384), BF16),
            vmem((768, cols), BF16),
            vmem((chunk * own, 384), F32),
            vmem((2, rows, 128), F32),
            vmem((2, 2, rows, 128), jnp.int32),
            vmem((2, 2, full, 128), F32),
            vmem((2, 2, full, 128), F32),
            vmem((14, 3, full, 128), F32),
            vmem((3, full, 6, 8, 128), F32),
            vmem((rows, 2, 8, 128), F32),
            vmem((nd, rows // nd, 2, 8, 128), F32),
            vmem((3, 8, kk * nd), F32),
            vmem((3, most, 8, kk * nd), F32),
            vmem((nd, CHUNKS, 2, 8, quarter, 128), F32),
            dma((14,)),
            dma((2, 2)),
            dma((2, 2)),
            dma((2, 2)),
            dma((2, 2)),
            dma((2, 4)),
            dma((2, 4)),
            dma((CHUNKS, nd)),
            dma((CHUNKS, nd)),
            dma((CHUNKS,)),
            dma((3, most)),
            dma((3, most)),
            dma((CHUNKS, nd, 2)),
            dma((CHUNKS, nd, 2)),
            dma((CHUNKS, 2)),
        ],
        compiler_params=pltpu.CompilerParams(
            collective_id=0, has_side_effects=True, vmem_limit_bytes=62 << 20
        ),
        name="sketch",
    )(directions, velocity, viscosity, basal_drag, misfit_weight, ice_mask, grounded)
    return pl.pallas_call(
        hand_over,
        out_shape=(
            jax.ShapeDtypeStruct((own, rows, cols), F32),
            jax.ShapeDtypeStruct((kk, kk), F32),
        ),
        in_specs=[any_space] * 2,
        out_specs=(any_space, any_space),
        scratch_shapes=[
            vmem((own, rows, cols), F32),
            vmem((kk, kk), F32),
            dma((own + 1,)),
            dma((own + 1,)),
        ],
        compiler_params=pltpu.CompilerParams(vmem_limit_bytes=62 << 20),
        name="hand_over",
    )(basis, upper)


def solution(mesh):
    placed = (P("dir", "gx", "gy"), P(None, "gx", "gy")) + (P("gx", "gy"),) * 5
    return jax.shard_map(
        functools.partial(on_device, mesh),
        mesh=mesh,
        in_specs=placed,
        out_specs=(P("dir", "gx", "gy"), P()),
        check_vma=False,
    )
```
